32 devices in a mesh: expert: 8 (over z, y), tensor: 4 (over x, core).
Axes of the slice: x: 2, y: 2, z: 4, core: 2. Of those that a mesh axis runs over, the one named last changes fastest.
Arguments:
- tokens: bfloat16 [1024, 7168], P('expert', 'tensor'), may hold values from -6 to 6
- out_grad: bfloat16 [1024, 7168], P('expert', 'tensor'), may hold values from -1.5 to 1.5
- expert_ids: int32 [1024, 2], P('expert'), may hold values from 0 to 7, all different within a row; in each aligned block of 128 rows (0 to 127, 128 to 255, ...) at most 48 rows name the same one
- gate_values: bfloat16 [1024, 2], P('expert'), may hold values from 0.099609375 to 1
- w_gate: bfloat16 [8, 7168, 1024], P('expert', None, 'tensor'), may hold values from -0.0625 to 0.0625
- w_up: bfloat16 [8, 7168, 1024], P('expert', None, 'tensor'), may hold values from -0.0625 to 0.0625
- w_down: bfloat16 [8, 1024, 7168], P('expert', 'tensor'), may hold values from -0.1875 to 0.1875
Outputs:
- d_tokens: bfloat16 [1024, 7168], P('expert', 'tensor')
- d_gates: float32 [1024, 2], P('expert')
The draws below stay inside these ranges and needn't reach their ends.
Inputs may be any that keep to these rules, and one draw needn't show every extreme that they name: `expert_ids`: each row names 2 different experts. Among the 128 rows held at one index along `expert` (one aligned block) no expert is named by more than 48 rows, and in some such block one expert is named by exactly 48.
All inputs are finite; a program needn't handle non-finite values.
Results may differ from the reference program's by a relative error of at most 0.0049.
Values may be sent and summed in bfloat16 or wider, within the bound.
A program may use at most 128 MiB of HBM per device.

```python
import math
import jax
import jax.numpy as jnp
import numpy as np
from jax import lax

D = 7168
FF = 1024
TOP = 2
TOK_GRP = 128
EXPERTS = 8
MOST = 48
TOKENS = 1024
N_EXPERT = 8


def steps_of(rng, shape, pieces, least, top_value):
    factor_of = 1.0
    for axis_at, shards_of in pieces:
        steps = jax.random.uniform(jax.random.fold_in(jax.random.fold_in(rng, 6), axis_at), (shards_of,), jnp.float32, least / len(pieces), top_value / len(pieces))
        factor_of = factor_of * jnp.repeat(jnp.exp(steps), shape[axis_at] // shards_of).reshape((-1,) + (1,) * (len(shape) - 1 - axis_at))
    return factor_of


def routed_block(own_key, own, number, rows, count, top, limit, lean):
    order = jax.random.permutation(own_key, count)
    packed, common = shares(count, rows * top, limit, lean, True), shares(count, rows * top, limit, lean, False)
    places = jnp.arange(count)

    def named(tallies, rotation):
        used = int((tallies > 0).sum())
        fixed = max(1, used // 4)
        shifted = fixed + (places - fixed + rotation * (used - fixed)) % max(1, count - fixed)
        return jnp.zeros((count,), jnp.int32).at[order[jnp.where(places < fixed, places, shifted)]].set(jnp.asarray(tallies, jnp.int32))

    tallies = jnp.where(number % 4 == 0, named(packed, number // 4), named(common, number - number // 4 - 1))
    mixed = jax.random.permutation(jax.random.fold_in(own, 3), count)
    donor, receiver = mixed[0:count // 2 * 2:2], mixed[1:count // 2 * 2:2]
    slack = jnp.minimum(tallies[donor] - 1, limit - tallies[receiver]) // 2
    slack = jnp.where((donor == order[0]) | (receiver == order[0]) | (tallies[receiver] == 0), 0, jnp.maximum(slack, 0))
    shifted = jax.random.randint(jax.random.fold_in(own, 4), (count // 2,), 0, 1 << 20) % (slack + 1)
    tallies = tallies.at[donor].add(-shifted).at[receiver].add(shifted)
    members = jnp.searchsorted(jnp.cumsum(tallies), jnp.arange(rows * top), side="right").astype(jnp.int32)
    listing = members.reshape(top, rows).T
    listing = listing[jax.random.permutation(jax.random.fold_in(own, 1), rows)]
    rotation = jax.random.randint(jax.random.fold_in(own, 2), (rows, 1), 0, top)
    return jnp.take_along_axis(listing, (jnp.arange(top)[None, :] + rotation) % top, axis=1)


def shares(count, total, limit, lean, full):
    weights = [(1 << 20) // math.isqrt(grade ** lean) + 1 for grade in range(1, count + 1)]
    largest = limit if full else min(limit, max(-(-total // count), total * weights[0] // sum(weights)))
    least = 1 if total - largest >= count - 1 else 0
    given, rest = [largest] + [least] * (count - 1), total - largest - least * (count - 1)
    while rest > 0:
        free = [i for i in range(1, count) if given[i] < largest] or [i for i in range(1, count) if given[i] < limit]
        whole, remaining = sum([weights[i] for i in free]), rest
        for i in free:
            more = min(limit - given[i], max(1, remaining * weights[i] // whole), rest)
            given[i] = given[i] + more
            rest = rest - more
    return np.array(given)


def scatter_about(key, extent, spread, reach, cuts=(), kind=jnp.bfloat16):
    result = spread * jax.random.normal(key, extent, jnp.float32)
    if cuts:
        result = result * steps_of(key, extent, cuts, -0.22, 0.18)
    return jnp.clip(result, -reach, reach).astype(kind)


def setup_inputs(seed: int = 0) -> dict:
    keys = jax.random.split(jax.random.key(seed), 8)
    tokens = scatter_about(keys[0], (TOKENS, D), 1.0, 6.0, ((0, 8), (1, 4)))
    out_grad = scatter_about(keys[1], (TOKENS, D), 0.25, 1.5, ((0, 8), (1, 4)))
    expert_ids_keys = jax.random.split(jax.random.fold_in(keys[2], 1), TOKENS // TOK_GRP)
    expert_ids_turns = jax.random.permutation(jax.random.fold_in(keys[2], 3), TOKENS // TOK_GRP)
    expert_ids = jax.vmap(lambda own, number: routed_block(jax.random.fold_in(keys[2], 2), own, number, TOK_GRP, EXPERTS, TOP, MOST, 2))(expert_ids_keys, expert_ids_turns).reshape((TOKENS, TOP))
    gate_values = jnp.clip(0.099609375 + 0.9003906 * jax.random.uniform(keys[3], (TOKENS, TOP), jnp.float32) ** steps_of(keys[3], (TOKENS, TOP), ((0, 8),), -0.2, 0.2), 0.099609375, 1.0).astype(jnp.bfloat16)
    w_gate = scatter_about(keys[4], (EXPERTS, D, FF), D ** -0.5, 0.0625, ((0, 8), (2, 4)))
    w_up = scatter_about(keys[5], (EXPERTS, D, FF), D ** -0.5, 0.0625, ((0, 8), (2, 4)))
    w_down = scatter_about(keys[6], (EXPERTS, FF, D), FF ** -0.5, 0.1875, ((0, 8), (1, 4)))
    return dict(tokens=tokens, out_grad=out_grad, expert_ids=expert_ids, gate_values=gate_values, w_gate=w_gate, w_up=w_up, w_down=w_down)


def reference(tokens, out_grad, expert_ids, gate_values, w_gate, w_up, w_down):
    assign = TOK_GRP * TOP
    grouped = expert_ids.reshape(N_EXPERT, assign)
    onehot = (grouped[:, :, None] == jnp.arange(EXPERTS, dtype=jnp.int32)[None, None, :]).astype(jnp.int32)
    before = jnp.cumsum(onehot, axis=1) - onehot
    rank = jnp.sum(before * onehot, axis=2).astype(jnp.int32)
    source = jnp.broadcast_to(jnp.arange(N_EXPERT, dtype=jnp.int32)[:, None], (N_EXPERT, assign))
    position = (source * assign + jnp.arange(assign, dtype=jnp.int32)[None, :]).astype(jnp.int32)
    table = jnp.full((EXPERTS, N_EXPERT, MOST), -1, jnp.int32).at[grouped, source, rank].set(position)
    table = table.reshape(EXPERTS, N_EXPERT * MOST)
    gate_flat = gate_values.reshape(-1).astype(jnp.float32)

    def one_expert(totals, inputs):
        grad_acc, slot_acc = totals
        slots, gate_mat, up_mat, down_mat = inputs
        is_live = slots >= 0
        safe_pos = jnp.where(is_live, slots, 0).astype(jnp.int32)
        tok_index = (safe_pos // TOP).astype(jnp.int32)
        zero_bf = jnp.zeros((), jnp.bfloat16)
        rows_x = jnp.where(is_live[:, None], tokens[tok_index], zero_bf)
        rows_dy = jnp.where(is_live[:, None], out_grad[tok_index], zero_bf)
        weight_g = jnp.where(is_live, gate_flat[safe_pos], jnp.float32(0.0))
        pre_act = jnp.dot(rows_x, gate_mat, preferred_element_type=jnp.float32)
        up_proj = jnp.dot(rows_x, up_mat, preferred_element_type=jnp.float32)
        grad_hid = jnp.dot(rows_dy, down_mat.T, preferred_element_type=jnp.float32)
        sigma = jax.nn.sigmoid(pre_act)
        active = pre_act * sigma
        slot_grad = jnp.sum(active * up_proj * grad_hid, axis=1)
        scaled = weight_g[:, None] * grad_hid
        grad_up = (scaled * active).astype(jnp.bfloat16)
        grad_pre = (scaled * up_proj * sigma * (1.0 + pre_act * (1.0 - sigma))).astype(jnp.bfloat16)
        contrib = jnp.dot(grad_pre, gate_mat.T, preferred_element_type=jnp.float32)
        contrib = contrib + jnp.dot(grad_up, up_mat.T, preferred_element_type=jnp.float32)
        grad_acc = grad_acc.at[tok_index].add(jnp.where(is_live[:, None], contrib, jnp.float32(0.0)))
        slot_acc = slot_acc.at[safe_pos].add(jnp.where(is_live, slot_grad, jnp.float32(0.0)))
        return (grad_acc, slot_acc), None

    start_acc = (jnp.zeros((TOKENS, D), jnp.float32), jnp.zeros((TOKENS * TOP,), jnp.float32))
    (grad_acc, slot_acc), _ = lax.scan(one_expert, start_acc, (table, w_gate, w_up, w_down))
    return grad_acc.astype(jnp.bfloat16), slot_acc.reshape(TOKENS, TOP)
```

```python
import jax
import jax.numpy as jnp
from jax import lax
from jax.sharding import PartitionSpec as P


def local(tokens, out_grad, expert_ids, gate_values, w_gate, w_up, w_down):
    n_experts = lax.axis_size("expert")
    tok_rows, quarter = tokens.shape
    top_count = expert_ids.shape[1]
    most_slots = 3 * tok_rows * top_count // (2 * n_experts)
    slot_count = n_experts * most_slots
    flat_ids = expert_ids.reshape(-1)
    onehot = (flat_ids[:, None] == jnp.arange(n_experts, dtype=jnp.int32)[None, :]).astype(
        jnp.int32
    )
    before = jnp.cumsum(onehot, axis=0) - onehot
    rank = jnp.sum(before * onehot, axis=1)
    slot_of = (flat_ids * most_slots + rank).reshape(tok_rows, top_count)
    matches = slot_of[None, :, :] == jnp.arange(slot_count, dtype=jnp.int32)[:, None, None]
    chooser = jnp.any(matches, axis=2).astype(jnp.bfloat16)
    send_x = jnp.dot(chooser, tokens, preferred_element_type=jnp.float32).astype(jnp.bfloat16)
    send_dy = jnp.dot(chooser, out_grad, preferred_element_type=jnp.float32).astype(jnp.bfloat16)
    gate_wide = gate_values.astype(jnp.float32)[None, :, :]
    send_g = jnp.sum(jnp.where(matches, gate_wide, 0.0), axis=(1, 2)).astype(jnp.bfloat16)
    recv_x, recv_dy, recv_g = (
        lax.all_to_all(
            send_x.reshape(n_experts, most_slots, quarter),
            "expert",
            split_axis=0,
            concat_axis=0,
            tiled=True,
        ),
        lax.all_to_all(
            send_dy.reshape(n_experts, most_slots, quarter),
            "expert",
            split_axis=0,
            concat_axis=0,
            tiled=True,
        ),
        lax.all_to_all(
            send_g.reshape(n_experts, most_slots), "expert", split_axis=0, concat_axis=0, tiled=True
        ),
    )
    rows_x = recv_x.reshape(slot_count, quarter)
    rows_dy = recv_dy.reshape(slot_count, quarter)
    gate_mat = w_gate[0]
    up_mat = w_up[0]
    down_mat = w_down[0]
    piece_x = lax.all_gather(rows_x, "tensor", axis=1, tiled=True)
    piece_dy = lax.all_gather(rows_dy, "tensor", axis=1, tiled=True)
    pre_sum = jnp.dot(piece_x, gate_mat, preferred_element_type=jnp.float32)
    up_sum = jnp.dot(piece_x, up_mat, preferred_element_type=jnp.float32)
    grad_sum = lax.dot_general(
        piece_dy, down_mat, (((1,), (1,)), ((), ())), preferred_element_type=jnp.float32
    )
    sigma = jax.nn.sigmoid(pre_sum)
    active = pre_sum * sigma
    partial_grad = jnp.sum(active * up_sum * grad_sum, axis=1)
    weight_g = recv_g.reshape(slot_count).astype(jnp.float32)
    scaled = weight_g[:, None] * grad_sum
    grad_up = (scaled * active).astype(jnp.bfloat16)
    grad_pre = (scaled * up_sum * sigma * (1.0 + pre_sum * (1.0 - sigma))).astype(jnp.bfloat16)
    contrib = lax.dot_general(
        grad_pre, gate_mat, (((1,), (1,)), ((), ())), preferred_element_type=jnp.float32
    )
    contrib = contrib + lax.dot_general(
        grad_up, up_mat, (((1,), (1,)), ((), ())), preferred_element_type=jnp.float32
    )
    slot_grad = lax.psum(partial_grad, "tensor")
    shares = lax.psum_scatter(
        contrib.astype(jnp.bfloat16), "tensor", scatter_dimension=1, tiled=True
    )
    returned = lax.all_to_all(
        shares.reshape(n_experts, most_slots, quarter),
        "expert",
        split_axis=0,
        concat_axis=0,
        tiled=True,
    )
    returned_grad = lax.all_to_all(
        slot_grad.reshape(n_experts, most_slots),
        "expert",
        split_axis=0,
        concat_axis=0,
        tiled=True,
    )
    d_tokens = lax.dot_general(
        chooser,
        returned.reshape(slot_count, quarter),
        (((0,), (0,)), ((), ())),
        preferred_element_type=jnp.float32,
    ).astype(jnp.bfloat16)
    grad_wide = returned_grad.reshape(slot_count)[:, None, None]
    d_gates = jnp.sum(jnp.where(matches, grad_wide, 0.0), axis=0)
    return (d_tokens, d_gates)


def solution(mesh):
    placed = (
        P("expert", "tensor"),
        P("expert", "tensor"),
        P("expert", None),
        P("expert", None),
        P("expert", None, "tensor"),
        P("expert", None, "tensor"),
        P("expert", "tensor", None),
    )
    return jax.shard_map(
        local,
        mesh=mesh,
        in_specs=placed,
        out_specs=(P("expert", "tensor"), P("expert", None)),
        check_vma=False,
    )
```

```python
import functools

import jax
import jax.numpy as jnp
from jax import lax
from jax.experimental import pallas as pl
from jax.experimental.pallas import tpu as pltpu
from jax.sharding import PartitionSpec as P


MESH = pl.DeviceIdType.MESH
VMEM = pl.BlockSpec(memory_space=pltpu.VMEM)
VMEM_BYTES = 56 * 1024 * 1024


def positions(n):
    me = lax.axis_index("expert")
    share = lax.axis_index("tensor")
    pair, side = share // 2, share % 2
    return me, share, pair * 2 + 1 - side, (1 - pair) * 2 + side


def greet(n, me, share, near, far):
    barrier = pltpu.get_barrier_semaphore()

    @pl.loop(1, n)
    def _(step):
        pl.semaphore_signal(
            barrier, inc=1, device_id=(lax.rem(me + step, n), share), device_id_type=MESH
        )

    for peer in (near, far):
        pl.semaphore_signal(barrier, inc=1, device_id=(me, peer), device_id_type=MESH)
    pl.semaphore_wait(barrier, n + 1)


def remote(src, dst, sems, index, device):
    return pltpu.make_async_remote_copy(
        src_ref=src,
        dst_ref=dst,
        send_sem=sems[0].at[index],
        recv_sem=sems[1].at[index],
        device_id=device,
        device_id_type=MESH,
    )


def spread_kernel(n, x_ref, dy_ref, g_ref, x_out, dy_out, g_out, *sems):
    me, share, near, far = positions(n)
    quarter = x_ref.shape[2]
    by_group, to_near, to_far, passed, gates = (sems[2 * i : 2 * i + 2] for i in range(5))
    own = sems[10]
    pairs = ((x_ref, x_out), (dy_ref, dy_out))

    def cols(which):
        return pl.ds(pl.multiple_of(which * quarter, 128), quarter)

    def block(which, group, owner):
        return pairs[which][1].at[group, :, cols(owner)]

    def dispatch(which, source, target):
        return remote(
            pairs[which][0].at[target],
            block(which, source, share),
            by_group,
            which * n + source,
            (target, share),
        )

    def gate_copy(source, target):
        return remote(
            g_ref.at[target], g_out.at[source], gates, source, (target, share)
        )

    def along(which, group, sent, sems_of, peer):
        return remote(
            block(which, group, sent),
            block(which, group, sent),
            sems_of,
            which * n + group,
            (me, peer),
        )

    greet(n, me, share, near, far)
    own_copies = [
        pltpu.make_async_copy(src.at[me], block(which, me, share), own.at[which])
        for which, (src, _) in enumerate(pairs)
    ]
    own_copies.append(pltpu.make_async_copy(g_ref.at[me], g_out.at[me], own.at[2]))
    for copy in own_copies:
        copy.start()
    for which in range(2):

        @pl.loop(1, n)
        def _(step):
            target = lax.rem(me + step, n)
            dispatch(which, me, target).start()

    @pl.loop(1, n)
    def _(step):
        gate_copy(me, lax.rem(me + step, n)).start()

    for copy in own_copies:
        copy.wait()

    def share_out(which, group):
        along(which, group, share, to_far, far).start()
        along(which, group, share, to_near, near).start()

    def pass_on(which, group):
        along(which, group, far, to_far, far).wait_recv()
        along(which, group, far, passed, near).start()

    for which in range(2):
        share_out(which, me)

        @pl.loop(1, n)
        def _(step):
            group = lax.rem(me - step + n, n)
            dispatch(which, group, me).wait_recv()
            share_out(which, group)
            pass_on(which, lax.rem(me - step + 1 + n, n))

        pass_on(which, lax.rem(me + 1, n))
    for which in range(2):

        @pl.loop(0, n)
        def _(group):
            along(which, group, near, to_near, near).wait_recv()
            along(which, group, 3 - share, passed, near).wait_recv()
            along(which, group, share, to_far, far).wait_send()
            along(which, group, share, to_near, near).wait_send()
            along(which, group, far, passed, near).wait_send()

        @pl.loop(1, n)
        def _(step):
            dispatch(which, me, lax.rem(me + step, n)).wait_send()

    @pl.loop(1, n)
    def _(step):
        gate_copy(me, lax.rem(me + step, n)).wait_send()
        gate_copy(lax.rem(me - step + n, n), me).wait_recv()


def spread(send_x, send_dy, send_g):
    n, most, quarter = send_x.shape
    wide = jax.ShapeDtypeStruct((n, most, 4 * quarter), send_x.dtype)
    dma = pltpu.SemaphoreType.DMA
    return pl.pallas_call(
        functools.partial(spread_kernel, n),
        out_shape=(wide, wide, jax.ShapeDtypeStruct(send_g.shape, send_g.dtype)),
        in_specs=[VMEM] * 3,
        out_specs=[VMEM] * 3,
        scratch_shapes=[dma((2 * n,))] * 8 + [dma((n,)), dma((n,)), dma((3,))],
        compiler_params=pltpu.CompilerParams(
            collective_id=0, has_side_effects=True, vmem_limit_bytes=VMEM_BYTES
        ),
    )(send_x, send_dy, send_g)


def collect_kernel(n, c_ref, p_ref, out, grad_out, near_got, far_put, far_got, put, total,
                   part_got, part_sum, *sems):
    me, share, near, far = positions(n)
    quarter = out.shape[2]
    to_near, to_far, back, grads, parts = (sems[2 * i : 2 * i + 2] for i in range(5))
    own = sems[10]

    def cols(which):
        return pl.ds(pl.multiple_of(which * quarter, 128), quarter)

    def half(group, slot):
        wanted = near if slot == 1 else 3 - share
        return remote(
            c_ref.at[group, :, cols(wanted)],
            near_got.at[group, slot],
            to_near,
            group * 2 + slot,
            (me, near),
        )

    def across(group):
        return remote(far_put.at[group], far_got.at[group], to_far, group, (me, far))

    def home(source, target):
        return remote(put.at[target], out.at[source], back, source, (target, share))

    def grad_home(source, target):
        return remote(
            part_sum.at[target], grad_out.at[source], grads, source, (target, share)
        )

    greet(n, me, share, near, far)
    part_near = remote(p_ref, part_got.at[0], parts, 0, (me, near))
    part_near.start()

    @pl.loop(0, n)
    def _(step):
        group = lax.rem(me + 1 + step, n)
        half(group, 0).start()
        half(group, 1).start()

    part_near.wait()
    part_sum[...] = p_ref[...] + part_got[0]
    part_far = remote(part_sum, part_got.at[1], parts, 1, (me, far))
    part_far.start()
    part_far.wait()
    part_sum[...] = part_sum[...] + part_got[1]

    @pl.loop(1, n)
    def _(step):
        grad_home(me, lax.rem(me + step, n)).start()

    def pair_sum(group):
        half(group, 0).wait_recv()
        mine = c_ref[group, :, cols(far)].astype(jnp.float32)
        far_put[group] = (mine + near_got[group, 0].astype(jnp.float32)).astype(far_put.dtype)
        across(group).start()
        half(group, 1).wait_recv()
        mine = c_ref[group, :, cols(share)].astype(jnp.float32)
        total[group] = mine + near_got[group, 1].astype(jnp.float32)

    def full_sum(group):
        across(group).wait_recv()
        put[group] = (total[group] + far_got[group].astype(jnp.float32)).astype(put.dtype)

    def send_home(group):
        full_sum(group)
        home(me, group).start()

    pair_sum(lax.rem(me + 1, n))

    @pl.loop(2, n + 1)
    def _(step):
        pair_sum(lax.rem(me + step, n))
        send_home(lax.rem(me + step - 1, n))

    full_sum(me)
    own_copies = [
        pltpu.make_async_copy(put.at[me], out.at[me], own.at[0]),
        pltpu.make_async_copy(part_sum.at[me], grad_out.at[me], own.at[1]),
    ]
    for copy in own_copies:
        copy.start()
    for copy in own_copies:
        copy.wait()

    @pl.loop(0, n)
    def _(group):
        half(group, 0).wait_send()
        half(group, 1).wait_send()
        across(group).wait_send()

    @pl.loop(1, n)
    def _(step):
        target = lax.rem(me + step, n)
        source = lax.rem(me - step + n, n)
        home(me, target).wait_send()
        grad_home(me, target).wait_send()
        home(source, me).wait_recv()
        grad_home(source, me).wait_recv()


def collect(contrib, partial_grad):
    n, most, width = contrib.shape
    quarter = width // 4
    kind = contrib.dtype
    dma = pltpu.SemaphoreType.DMA
    stage = pltpu.VMEM((n, most, quarter), kind)
    return pl.pallas_call(
        functools.partial(collect_kernel, n),
        out_shape=(
            jax.ShapeDtypeStruct((n, most, quarter), kind),
            jax.ShapeDtypeStruct(partial_grad.shape, partial_grad.dtype),
        ),
        in_specs=[VMEM] * 2,
        out_specs=[VMEM] * 2,
        scratch_shapes=[
            pltpu.VMEM((n, 2, most, quarter), kind),
            stage,
            stage,
            stage,
            pltpu.VMEM((n, most, quarter), jnp.float32),
            pltpu.VMEM((2,) + partial_grad.shape, jnp.float32),
            pltpu.VMEM(partial_grad.shape, jnp.float32),
            dma((2 * n,)),
            dma((2 * n,)),
        ]
        + [dma((n,))] * 6
        + [dma((2,)), dma((2,)), dma((2,))],
        compiler_params=pltpu.CompilerParams(
            collective_id=1, has_side_effects=True, vmem_limit_bytes=VMEM_BYTES
        ),
    )(contrib, partial_grad)


def local(tokens, out_grad, expert_ids, gate_values, w_gate, w_up, w_down):
    n_experts = lax.axis_size("expert")
    tok_rows, quarter = tokens.shape
    top_count = expert_ids.shape[1]
    most_slots = 3 * tok_rows * top_count // (2 * n_experts)
    slot_count = n_experts * most_slots
    flat_ids = expert_ids.reshape(-1)
    onehot = (flat_ids[:, None] == jnp.arange(n_experts, dtype=jnp.int32)[None, :]).astype(
        jnp.int32
    )
    before = jnp.cumsum(onehot, axis=0) - onehot
    rank = jnp.sum(before * onehot, axis=1)
    slot_of = (flat_ids * most_slots + rank).reshape(tok_rows, top_count)
    matches = slot_of[None, :, :] == jnp.arange(slot_count, dtype=jnp.int32)[:, None, None]
    chooser = jnp.any(matches, axis=2).astype(jnp.bfloat16)
    send_x = jnp.dot(chooser, tokens, preferred_element_type=jnp.float32).astype(jnp.bfloat16)
    send_dy = jnp.dot(chooser, out_grad, preferred_element_type=jnp.float32).astype(jnp.bfloat16)
    gate_wide = gate_values.astype(jnp.float32)[None, :, :]
    send_g = jnp.sum(jnp.where(matches, gate_wide, 0.0), axis=(1, 2))
    piece_x, piece_dy, recv_g = spread(
        send_x.reshape(n_experts, most_slots, quarter),
        send_dy.reshape(n_experts, most_slots, quarter),
        send_g.reshape(n_experts, 1, most_slots),
    )
    piece_x = piece_x.reshape(slot_count, 4 * quarter)
    piece_dy = piece_dy.reshape(slot_count, 4 * quarter)
    gate_mat = w_gate[0]
    up_mat = w_up[0]
    down_mat = w_down[0]
    pre_sum = jnp.dot(piece_x, gate_mat, preferred_element_type=jnp.float32)
    up_sum = jnp.dot(piece_x, up_mat, preferred_element_type=jnp.float32)
    grad_sum = lax.dot_general(
        piece_dy, down_mat, (((1,), (1,)), ((), ())), preferred_element_type=jnp.float32
    )
    sigma = jax.nn.sigmoid(pre_sum)
    active = pre_sum * sigma
    partial_grad = jnp.sum(active * up_sum * grad_sum, axis=1)
    weight_g = recv_g.reshape(slot_count)
    scaled = weight_g[:, None] * grad_sum
    grad_up = (scaled * active).astype(jnp.bfloat16)
    grad_pre = (scaled * up_sum * sigma * (1.0 + pre_sum * (1.0 - sigma))).astype(jnp.bfloat16)
    contrib = lax.dot_general(
        grad_pre, gate_mat, (((1,), (1,)), ((), ())), preferred_element_type=jnp.float32
    )
    contrib = contrib + lax.dot_general(
        grad_up, up_mat, (((1,), (1,)), ((), ())), preferred_element_type=jnp.float32
    )
    returned, returned_grad = collect(
        contrib.astype(jnp.bfloat16).reshape(n_experts, most_slots, 4 * quarter),
        partial_grad.reshape(n_experts, 1, most_slots),
    )
    d_tokens = lax.dot_general(
        chooser,
        returned.reshape(slot_count, quarter),
        (((0,), (0,)), ((), ())),
        preferred_element_type=jnp.float32,
    ).astype(jnp.bfloat16)
    grad_wide = returned_grad.reshape(slot_count)[:, None, None]
    d_gates = jnp.sum(jnp.where(matches, grad_wide, 0.0), axis=0)
    return (d_tokens, d_gates)


def solution(mesh):
    placed = (
        P("expert", "tensor"),
        P("expert", "tensor"),
        P("expert", None),
        P("expert", None),
        P("expert", None, "tensor"),
        P("expert", None, "tensor"),
        P("expert", "tensor", None),
    )
    return jax.shard_map(
        local,
        mesh=mesh,
        in_specs=placed,
        out_specs=(P("expert", "tensor"), P("expert", None)),
        check_vma=False,
    )
```

```python
import functools

import jax
import jax.numpy as jnp
from jax import lax
from jax.experimental import pallas as pl
from jax.experimental.pallas import tpu as pltpu
from jax.sharding import PartitionSpec as P


MESH = pl.DeviceIdType.MESH
VMEM = pl.BlockSpec(memory_space=pltpu.VMEM)
VMEM_BYTES = 56 * 1024 * 1024


def positions(n):
    me = lax.axis_index("expert")
    share = lax.axis_index("tensor")
    pair, side = share // 2, share % 2
    return me, share, pair * 2 + 1 - side, (1 - pair) * 2 + side


def greet(n, me, share, near, far):
    barrier = pltpu.get_barrier_semaphore()

    @pl.loop(1, n)
    def _(step):
        pl.semaphore_signal(
            barrier, inc=1, device_id=(lax.rem(me + step, n), share), device_id_type=MESH
        )

    for peer in (near, far):
        pl.semaphore_signal(barrier, inc=1, device_id=(me, peer), device_id_type=MESH)
    pl.semaphore_wait(barrier, n + 1)


def remote(src, dst, sems, index, device):
    return pltpu.make_async_remote_copy(
        src_ref=src,
        dst_ref=dst,
        send_sem=sems[0].at[index],
        recv_sem=sems[1].at[index],
        device_id=device,
        device_id_type=MESH,
    )


def spread_kernel(n, x_ref, dy_ref, g_ref, x_out, dy_out, g_out, *sems):
    me, share, near, far = positions(n)
    quarter = x_ref.shape[2]
    by_group, to_near, to_far, passed, gates = (sems[2 * i : 2 * i + 2] for i in range(5))
    own = sems[10]
    pairs = ((x_ref, x_out), (dy_ref, dy_out))

    def cols(which):
        return pl.ds(pl.multiple_of(which * quarter, 128), quarter)

    def block(which, group, owner):
        return pairs[which][1].at[group, :, cols(owner)]

    def dispatch(which, source, target):
        return remote(
            pairs[which][0].at[target],
            block(which, source, share),
            by_group,
            which * n + source,
            (target, share),
        )

    def gate_copy(source, target):
        return remote(
            g_ref.at[target], g_out.at[source], gates, source, (target, share)
        )

    def along(which, group, sent, sems_of, peer):
        return remote(
            block(which, group, sent),
            block(which, group, sent),
            sems_of,
            which * n + group,
            (me, peer),
        )

    greet(n, me, share, near, far)
    own_copies = [
        pltpu.make_async_copy(src.at[me], block(which, me, share), own.at[which])
        for which, (src, _) in enumerate(pairs)
    ]
    own_copies.append(pltpu.make_async_copy(g_ref.at[me], g_out.at[me], own.at[2]))
    for copy in own_copies:
        copy.start()
    for which in range(2):

        @pl.loop(1, n)
        def _(step):
            target = lax.rem(me + step, n)
            dispatch(which, me, target).start()

    @pl.loop(1, n)
    def _(step):
        gate_copy(me, lax.rem(me + step, n)).start()

    for copy in own_copies:
        copy.wait()

    def share_out(which, group):
        along(which, group, share, to_far, far).start()
        along(which, group, share, to_near, near).start()

    def pass_on(which, group):
        along(which, group, far, to_far, far).wait_recv()
        along(which, group, far, passed, near).start()

    for which in range(2):
        share_out(which, me)

        @pl.loop(1, n)
        def _(step):
            group = lax.rem(me - step + n, n)
            dispatch(which, group, me).wait_recv()
            share_out(which, group)
            pass_on(which, lax.rem(me - step + 1 + n, n))

        pass_on(which, lax.rem(me + 1, n))
    for which in range(2):

        @pl.loop(0, n)
        def _(group):
            along(which, group, near, to_near, near).wait_recv()
            along(which, group, 3 - share, passed, near).wait_recv()
            along(which, group, share, to_far, far).wait_send()
            along(which, group, share, to_near, near).wait_send()
            along(which, group, far, passed, near).wait_send()

        @pl.loop(1, n)
        def _(step):
            dispatch(which, me, lax.rem(me + step, n)).wait_send()

    @pl.loop(1, n)
    def _(step):
        gate_copy(me, lax.rem(me + step, n)).wait_send()
        gate_copy(lax.rem(me - step + n, n), me).wait_recv()


def spread(send_x, send_dy, send_g):
    n, most, quarter = send_x.shape
    wide = jax.ShapeDtypeStruct((n, most, 4 * quarter), send_x.dtype)
    dma = pltpu.SemaphoreType.DMA
    return pl.pallas_call(
        functools.partial(spread_kernel, n),
        out_shape=(wide, wide, jax.ShapeDtypeStruct(send_g.shape, send_g.dtype)),
        in_specs=[VMEM] * 3,
        out_specs=[VMEM] * 3,
        scratch_shapes=[dma((2 * n,))] * 8 + [dma((n,)), dma((n,)), dma((3,))],
        compiler_params=pltpu.CompilerParams(
            collective_id=0, has_side_effects=True, vmem_limit_bytes=VMEM_BYTES
        ),
    )(send_x, send_dy, send_g)


def collect_kernel(n, c_ref, p_ref, out, grad_out, near_got, far_put, far_got, put, total,
                   part_got, part_sum, *sems):
    me, share, near, far = positions(n)
    quarter = out.shape[2]
    to_near, to_far, back, grads, parts = (sems[2 * i : 2 * i + 2] for i in range(5))
    own = sems[10]

    def cols(which):
        return pl.ds(pl.multiple_of(which * quarter, 128), quarter)

    def half(group, slot):
        wanted = near if slot == 1 else 3 - share
        return remote(
            c_ref.at[group, :, cols(wanted)],
            near_got.at[group, slot],
            to_near,
            group * 2 + slot,
            (me, near),
        )

    def across(group):
        return remote(far_put.at[group], far_got.at[group], to_far, group, (me, far))

    def home(source, target):
        return remote(put.at[target], out.at[source], back, source, (target, share))

    def grad_home(source, target):
        return remote(
            part_sum.at[target], grad_out.at[source], grads, source, (target, share)
        )

    greet(n, me, share, near, far)
    part_near = remote(p_ref, part_got.at[0], parts, 0, (me, near))
    part_near.start()

    @pl.loop(0, n)
    def _(step):
        group = lax.rem(me + 1 + step, n)
        half(group, 0).start()
        half(group, 1).start()

    part_near.wait()
    part_sum[...] = p_ref[...] + part_got[0]
    part_far = remote(part_sum, part_got.at[1], parts, 1, (me, far))
    part_far.start()
    part_far.wait()
    part_sum[...] = part_sum[...] + part_got[1]

    @pl.loop(1, n)
    def _(step):
        grad_home(me, lax.rem(me + step, n)).start()

    def pair_sum(group):
        half(group, 0).wait_recv()
        mine = c_ref[group, :, cols(far)].astype(jnp.float32)
        far_put[group] = (mine + near_got[group, 0].astype(jnp.float32)).astype(far_put.dtype)
        across(group).start()
        half(group, 1).wait_recv()
        mine = c_ref[group, :, cols(share)].astype(jnp.float32)
        total[group] = mine + near_got[group, 1].astype(jnp.float32)

    def full_sum(group):
        across(group).wait_recv()
        put[group] = (total[group] + far_got[group].astype(jnp.float32)).astype(put.dtype)

    def send_home(group):
        full_sum(group)
        home(me, group).start()

    pair_sum(lax.rem(me + 1, n))

    @pl.loop(2, n + 1)
    def _(step):
        pair_sum(lax.rem(me + step, n))
        send_home(lax.rem(me + step - 1, n))

    full_sum(me)
    own_copies = [
        pltpu.make_async_copy(put.at[me], out.at[me], own.at[0]),
        pltpu.make_async_copy(part_sum.at[me], grad_out.at[me], own.at[1]),
    ]
    for copy in own_copies:
        copy.start()
    for copy in own_copies:
        copy.wait()

    @pl.loop(0, n)
    def _(group):
        half(group, 0).wait_send()
        half(group, 1).wait_send()
        across(group).wait_send()

    @pl.loop(1, n)
    def _(step):
        target = lax.rem(me + step, n)
        source = lax.rem(me - step + n, n)
        home(me, target).wait_send()
        grad_home(me, target).wait_send()
        home(source, me).wait_recv()
        grad_home(source, me).wait_recv()


def collect(contrib, partial_grad):
    n, most, width = contrib.shape
    quarter = width // 4
    kind = contrib.dtype
    dma = pltpu.SemaphoreType.DMA
    stage = pltpu.VMEM((n, most, quarter), kind)
    return pl.pallas_call(
        functools.partial(collect_kernel, n),
        out_shape=(
            jax.ShapeDtypeStruct((n, most, quarter), kind),
            jax.ShapeDtypeStruct(partial_grad.shape, partial_grad.dtype),
        ),
        in_specs=[VMEM] * 2,
        out_specs=[VMEM] * 2,
        scratch_shapes=[
            pltpu.VMEM((n, 2, most, quarter), kind),
            stage,
            stage,
            stage,
            pltpu.VMEM((n, most, quarter), jnp.float32),
            pltpu.VMEM((2,) + partial_grad.shape, jnp.float32),
            pltpu.VMEM(partial_grad.shape, jnp.float32),
            dma((2 * n,)),
            dma((2 * n,)),
        ]
        + [dma((n,))] * 6
        + [dma((2,)), dma((2,)), dma((2,))],
        compiler_params=pltpu.CompilerParams(
            collective_id=1, has_side_effects=True, vmem_limit_bytes=VMEM_BYTES
        ),
    )(contrib, partial_grad)


def fused_kernel(n, x_ref, dy_ref, g_ref, gate_hbm, up_hbm, down_hbm, out, grad_out,
                 x_out, dy_out, g_out, gate_w, up_w, down_w, pre, up, dz, dp, du,
                 near_put, mine, near_got, far_put, far_got, put, part, part_got, part_sum,
                 load, *all_sems):
    sems, late = all_sems[:11], all_sems[11:]
    me, share, near, far = positions(n)
    quarter = x_ref.shape[2]
    by_group, to_near, to_far, passed, gates = (sems[2 * i : 2 * i + 2] for i in range(5))
    own = sems[10]
    pairs = ((x_ref, x_out), (dy_ref, dy_out))

    def cols(which):
        return pl.ds(pl.multiple_of(which * quarter, 128), quarter)

    def block(which, group, owner):
        return pairs[which][1].at[group, :, cols(owner)]

    def dispatch(which, source, target):
        return remote(
            pairs[which][0].at[target],
            block(which, source, share),
            by_group,
            which * n + source,
            (target, share),
        )

    def gate_copy(source, target):
        return remote(
            g_ref.at[target], g_out.at[source], gates, source, (target, share)
        )

    def along(which, group, sent, sems_of, peer):
        return remote(
            block(which, group, sent),
            block(which, group, sent),
            sems_of,
            which * n + group,
            (me, peer),
        )

    to_pair, across_sems, back, grads, parts = (late[2 * i : 2 * i + 2] for i in range(5))
    most = x_ref.shape[1]
    rows = n * most
    depth = quarter // 2
    narrow = quarter // 7
    loads = [
        pltpu.make_async_copy(src, dst, load.at[i])
        for i, (src, dst) in enumerate(
            ((gate_hbm, gate_w), (up_hbm, up_w), (down_hbm, down_w))
        )
    ]

    def half(group, slot):
        return remote(
            near_put.at[slot, group],
            near_got.at[slot, group],
            to_pair,
            slot * n + group,
            (me, near),
        )

    def across(group):
        return remote(far_put.at[group], far_got.at[group], across_sems, group, (me, far))

    def home(source, target):
        return remote(put.at[target], out.at[source], back, source, (target, share))

    def grad_home(source, target):
        return remote(
            part_sum.at[target], grad_out.at[source], grads, source, (target, share)
        )

    def nt(left, right):
        return lax.dot_general(
            left, right, (((1,), (1,)), ((), ())), preferred_element_type=jnp.float32
        )

    def project(step):
        at = pl.ds(pl.multiple_of(step * depth, 128), depth)
        piece = x_out[:, :, at].reshape(rows, depth)
        pre[...] += jnp.dot(piece, gate_w[at, :], preferred_element_type=jnp.float32)
        up[...] += jnp.dot(piece, up_w[at, :], preferred_element_type=jnp.float32)

    greet(n, me, share, near, far)
    own_copies = [
        pltpu.make_async_copy(src.at[me], block(which, me, share), own.at[which])
        for which, (src, _) in enumerate(pairs)
    ]
    own_copies.append(pltpu.make_async_copy(g_ref.at[me], g_out.at[me], own.at[2]))
    for copy in own_copies:
        copy.start()
    for which in range(2):

        @pl.loop(1, n)
        def _(step):
            target = lax.rem(me + step, n)
            dispatch(which, me, target).start()

    @pl.loop(1, n)
    def _(step):
        gate_copy(me, lax.rem(me + step, n)).start()

    for copy in loads:
        copy.start()
    pre[...] = jnp.zeros_like(pre)
    up[...] = jnp.zeros_like(up)
    dz[...] = jnp.zeros_like(dz)
    for copy in own_copies:
        copy.wait()

    def share_out(which, group):
        along(which, group, share, to_far, far).start()
        along(which, group, share, to_near, near).start()

    def pass_on(which, group):
        along(which, group, far, to_far, far).wait_recv()
        along(which, group, far, passed, near).start()

    def settle(which):
        @pl.loop(0, n)
        def _(group):
            along(which, group, near, to_near, near).wait_recv()
            along(which, group, 3 - share, passed, near).wait_recv()

    share_out(0, me)

    @pl.loop(1, n)
    def _(step):
        group = lax.rem(me - step + n, n)
        dispatch(0, group, me).wait_recv()
        share_out(0, group)
        pass_on(0, lax.rem(me - step + 1 + n, n))

    share_out(1, me)
    pass_on(0, lax.rem(me + 1, n))
    settle(0)
    loads[0].wait()
    loads[1].wait()

    @pl.loop(1, n)
    def _(step):
        project(step - 1)
        group = lax.rem(me - step + n, n)
        dispatch(1, group, me).wait_recv()
        share_out(1, group)
        pass_on(1, lax.rem(me - step + 1 + n, n))

    @pl.loop(n - 1, 8)
    def _(step):
        project(step)

    pass_on(1, lax.rem(me + 1, n))

    @pl.loop(1, n)
    def _(step):
        gate_copy(lax.rem(me - step + n, n), me).wait_recv()

    loads[2].wait()
    settle(1)

    @pl.loop(0, 8)
    def _(step):
        at = pl.ds(pl.multiple_of(step * depth, 128), depth)
        dz[...] += nt(dy_out[:, :, at].reshape(rows, depth), down_w[:, at])

    @pl.loop(0, n)
    def _(group):
        at = pl.ds(pl.multiple_of(group * most, 16), most)
        pre_b, up_b, dz_b = pre[at, :], up[at, :], dz[at, :]
        sigma = jax.nn.sigmoid(pre_b)
        active = pre_b * sigma
        row = jnp.sum(active * up_b * dz_b, axis=1, keepdims=True)
        part[group] = jnp.broadcast_to(row, (most, 128))
        scaled = g_out[group][:, :1].astype(jnp.float32) * dz_b
        du[at, :] = (scaled * active).astype(du.dtype)
        dp[at, :] = (scaled * up_b * sigma * (1.0 + pre_b * (1.0 - sigma))).astype(dp.dtype)

    part_near = remote(part, part_got.at[0], parts, 0, (me, near))
    part_near.start()

    def expand(which, store):
        @pl.loop(0, 7)
        def _(step):
            at = pl.ds(pl.multiple_of(which * quarter + step * narrow, 128), narrow)
            value = nt(dp[...], gate_w[at, :]) + nt(du[...], up_w[at, :])
            store(
                pl.ds(pl.multiple_of(step * narrow, 128), narrow),
                value.reshape(n, most, narrow),
            )

    for slot, wanted in ((0, 3 - share), (1, near)):

        def keep(at, value):
            near_put[slot, :, :, at] = value.astype(near_put.dtype)

        expand(wanted, keep)

        @pl.loop(0, n)
        def _(step):
            half(lax.rem(me + 1 + step, n), slot).start()

    for slot, wanted in ((0, far), (1, share)):

        def keep_wide(at, value):
            mine[slot, :, :, at] = value

        expand(wanted, keep_wide)
        if slot == 0:
            part_near.wait()
            part_sum[...] = part[...] + part_got[0]
            part_far = remote(part_sum, part_got.at[1], parts, 1, (me, far))
            part_far.start()

            @pl.loop(0, n)
            def _(step):
                group = lax.rem(me + 1 + step, n)
                half(group, 0).wait_recv()
                far_put[group] = (
                    mine[0, group] + near_got[0, group].astype(jnp.float32)
                ).astype(far_put.dtype)
                across(group).start()

    part_far.wait()
    part_sum[...] = part_sum[...] + part_got[1]

    @pl.loop(1, n)
    def _(step):
        grad_home(me, lax.rem(me + step, n)).start()

    def full_sum(group):
        half(group, 1).wait_recv()
        across(group).wait_recv()
        pair = mine[1, group] + near_got[1, group].astype(jnp.float32)
        put[group] = (pair + far_got[group].astype(jnp.float32)).astype(put.dtype)

    @pl.loop(1, n)
    def _(step):
        group = lax.rem(me + step, n)
        full_sum(group)
        home(me, group).start()

    full_sum(me)
    last_copies = [
        pltpu.make_async_copy(put.at[me], out.at[me], own.at[0]),
        pltpu.make_async_copy(part_sum.at[me], grad_out.at[me], own.at[1]),
    ]
    for copy in last_copies:
        copy.start()
    for copy in last_copies:
        copy.wait()
    for which in range(2):

        @pl.loop(0, n)
        def _(group):
            along(which, group, share, to_far, far).wait_send()
            along(which, group, share, to_near, near).wait_send()
            along(which, group, far, passed, near).wait_send()
            half(group, which).wait_send()

        @pl.loop(1, n)
        def _(step):
            dispatch(which, me, lax.rem(me + step, n)).wait_send()

    @pl.loop(0, n)
    def _(group):
        across(group).wait_send()

    @pl.loop(1, n)
    def _(step):
        target = lax.rem(me + step, n)
        source = lax.rem(me - step + n, n)
        gate_copy(me, target).wait_send()
        home(me, target).wait_send()
        grad_home(me, target).wait_send()
        home(source, me).wait_recv()
        grad_home(source, me).wait_recv()


def fused(send_x, send_dy, send_g, gate_mat, up_mat, down_mat):
    n, most, quarter = send_x.shape
    kind = send_x.dtype
    hidden = gate_mat.shape[1]
    rows = n * most
    dma = pltpu.SemaphoreType.DMA
    wide = pltpu.VMEM((n, most, 4 * quarter), kind)
    square = pltpu.VMEM((rows, hidden), jnp.float32)
    stage = pltpu.VMEM((n, most, quarter), kind)
    flat = (n, most, 128)
    anywhere = pl.BlockSpec(memory_space=pl.ANY)
    return pl.pallas_call(
        functools.partial(fused_kernel, n),
        out_shape=(
            jax.ShapeDtypeStruct((n, most, quarter), kind),
            jax.ShapeDtypeStruct(flat, jnp.float32),
        ),
        in_specs=[VMEM] * 3 + [anywhere] * 3,
        out_specs=[VMEM] * 2,
        scratch_shapes=[
            wide,
            wide,
            pltpu.VMEM(flat, kind),
            pltpu.VMEM(gate_mat.shape, kind),
            pltpu.VMEM(up_mat.shape, kind),
            pltpu.VMEM(down_mat.shape, kind),
            square,
            square,
            square,
            pltpu.VMEM((rows, hidden), kind),
            pltpu.VMEM((rows, hidden), kind),
            pltpu.VMEM((2, n, most, quarter), kind),
            pltpu.VMEM((2, n, most, quarter), jnp.float32),
            pltpu.VMEM((2, n, most, quarter), kind),
            stage,
            stage,
            stage,
            pltpu.VMEM(flat, jnp.float32),
            pltpu.VMEM((2,) + flat, jnp.float32),
            pltpu.VMEM(flat, jnp.float32),
            dma((3,)),
        ]
        + [dma((2 * n,))] * 8
        + [dma((n,)), dma((n,)), dma((3,))]
        + [dma((2 * n,))] * 2
        + [dma((n,))] * 6
        + [dma((2,))] * 2,
        compiler_params=pltpu.CompilerParams(
            collective_id=2, has_side_effects=True, vmem_limit_bytes=VMEM_BYTES
        ),
    )(send_x, send_dy, send_g, gate_mat, up_mat, down_mat)


def in_steps(send_x, send_dy, send_g, gate_mat, up_mat, down_mat):
    n_experts, most_slots, quarter = send_x.shape
    slot_count = n_experts * most_slots
    piece_x, piece_dy, recv_g = spread(
        send_x,
        send_dy,
        send_g.reshape(n_experts, 1, most_slots),
    )
    piece_x = piece_x.reshape(slot_count, 4 * quarter)
    piece_dy = piece_dy.reshape(slot_count, 4 * quarter)
    pre_sum = jnp.dot(piece_x, gate_mat, preferred_element_type=jnp.float32)
    up_sum = jnp.dot(piece_x, up_mat, preferred_element_type=jnp.float32)
    grad_sum = lax.dot_general(
        piece_dy, down_mat, (((1,), (1,)), ((), ())), preferred_element_type=jnp.float32
    )
    sigma = jax.nn.sigmoid(pre_sum)
    active = pre_sum * sigma
    partial_grad = jnp.sum(active * up_sum * grad_sum, axis=1)
    weight_g = recv_g.reshape(slot_count)
    scaled = weight_g[:, None] * grad_sum
    grad_up = (scaled * active).astype(jnp.bfloat16)
    grad_pre = (scaled * up_sum * sigma * (1.0 + pre_sum * (1.0 - sigma))).astype(jnp.bfloat16)
    contrib = lax.dot_general(
        grad_pre, gate_mat, (((1,), (1,)), ((), ())), preferred_element_type=jnp.float32
    )
    contrib = contrib + lax.dot_general(
        grad_up, up_mat, (((1,), (1,)), ((), ())), preferred_element_type=jnp.float32
    )
    returned, returned_grad = collect(
        contrib.astype(jnp.bfloat16).reshape(n_experts, most_slots, 4 * quarter),
        partial_grad.reshape(n_experts, 1, most_slots),
    )
    return returned, returned_grad


def local(tokens, out_grad, expert_ids, gate_values, w_gate, w_up, w_down):
    n_experts = lax.axis_size("expert")
    tok_rows, quarter = tokens.shape
    top_count = expert_ids.shape[1]
    most_slots = 3 * tok_rows * top_count // (2 * n_experts)
    slot_count = n_experts * most_slots
    flat_ids = expert_ids.reshape(-1)
    onehot = (flat_ids[:, None] == jnp.arange(n_experts, dtype=jnp.int32)[None, :]).astype(
        jnp.int32
    )
    before = jnp.cumsum(onehot, axis=0) - onehot
    rank = jnp.sum(before * onehot, axis=1)
    slot_of = (flat_ids * most_slots + rank).reshape(tok_rows, top_count)
    matches = slot_of[None, :, :] == jnp.arange(slot_count, dtype=jnp.int32)[:, None, None]
    chooser = jnp.any(matches, axis=2).astype(jnp.bfloat16)
    send_x = jnp.dot(chooser, tokens, preferred_element_type=jnp.float32).astype(jnp.bfloat16)
    send_dy = jnp.dot(chooser, out_grad, preferred_element_type=jnp.float32).astype(jnp.bfloat16)
    gate_wide = gate_values.astype(jnp.float32)[None, :, :]
    send_g = jnp.sum(jnp.where(matches, gate_wide, 0.0), axis=(1, 2))
    send_x = send_x.reshape(n_experts, most_slots, quarter)
    send_dy = send_dy.reshape(n_experts, most_slots, quarter)
    weights = (w_gate[0], w_up[0], w_down[0])
    if most_slots % 16 == 0 and n_experts <= 9 and quarter % 1792 == 0:
        wide_g = jnp.broadcast_to(
            send_g.astype(jnp.bfloat16).reshape(n_experts, most_slots, 1),
            (n_experts, most_slots, 128),
        )
        returned, returned_grad = fused(send_x, send_dy, wide_g, *weights)
        returned_grad = returned_grad[:, :, 0]
    else:
        returned, returned_grad = in_steps(send_x, send_dy, send_g, *weights)
    d_tokens = lax.dot_general(
        chooser,
        returned.reshape(slot_count, quarter),
        (((0,), (0,)), ((), ())),
        preferred_element_type=jnp.float32,
    ).astype(jnp.bfloat16)
    grad_wide = returned_grad.reshape(slot_count)[:, None, None]
    d_gates = jnp.sum(jnp.where(matches, grad_wide, 0.0), axis=0)
    return (d_tokens, d_gates)


def solution(mesh):
    placed = (
        P("expert", "tensor"),
        P("expert", "tensor"),
        P("expert", None),
        P("expert", None),
        P("expert", None, "tensor"),
        P("expert", None, "tensor"),
        P("expert", "tensor", None),
    )
    return jax.shard_map(
        local,
        mesh=mesh,
        in_specs=placed,
        out_specs=(P("expert", "tensor"), P("expert", None)),
        check_vma=False,
    )
```

```python
import functools

import jax
import jax.numpy as jnp
from jax import lax
from jax.experimental import pallas as pl
from jax.experimental.pallas import tpu as pltpu
from jax.sharding import PartitionSpec as P


MESH = pl.DeviceIdType.MESH
VMEM = pl.BlockSpec(memory_space=pltpu.VMEM)
VMEM_BYTES = 56 * 1024 * 1024


def positions(n):
    me = lax.axis_index("expert")
    share = lax.axis_index("tensor")
    pair, side = share // 2, share % 2
    return me, share, pair * 2 + 1 - side, (1 - pair) * 2 + side


def greet(n, me, share, near, far):
    barrier = pltpu.get_barrier_semaphore()

    @pl.loop(1, n)
    def _(step):
        pl.semaphore_signal(
            barrier, inc=1, device_id=(lax.rem(me + step, n), share), device_id_type=MESH
        )

    for peer in (near, far):
        pl.semaphore_signal(barrier, inc=1, device_id=(me, peer), device_id_type=MESH)
    pl.semaphore_wait(barrier, n + 1)


def remote(src, dst, sems, index, device):
    return pltpu.make_async_remote_copy(
        src_ref=src,
        dst_ref=dst,
        send_sem=sems[0].at[index],
        recv_sem=sems[1].at[index],
        device_id=device,
        device_id_type=MESH,
    )


def spread_kernel(n, x_ref, dy_ref, g_ref, x_out, dy_out, g_out, *sems):
    me, share, near, far = positions(n)
    quarter = x_ref.shape[2]
    by_group, to_near, to_far, passed, gates = (sems[2 * i : 2 * i + 2] for i in range(5))
    own = sems[10]
    pairs = ((x_ref, x_out), (dy_ref, dy_out))

    def cols(which):
        return pl.ds(pl.multiple_of(which * quarter, 128), quarter)

    def block(which, group, owner):
        return pairs[which][1].at[group, :, cols(owner)]

    def dispatch(which, source, target):
        return remote(
            pairs[which][0].at[target],
            block(which, source, share),
            by_group,
            which * n + source,
            (target, share),
        )

    def gate_copy(source, target):
        return remote(
            g_ref.at[target], g_out.at[source], gates, source, (target, share)
        )

    def along(which, group, sent, sems_of, peer):
        return remote(
            block(which, group, sent),
            block(which, group, sent),
            sems_of,
            which * n + group,
            (me, peer),
        )

    greet(n, me, share, near, far)
    own_copies = [
        pltpu.make_async_copy(src.at[me], block(which, me, share), own.at[which])
        for which, (src, _) in enumerate(pairs)
    ]
    own_copies.append(pltpu.make_async_copy(g_ref.at[me], g_out.at[me], own.at[2]))
    for copy in own_copies:
        copy.start()
    for which in range(2):

        @pl.loop(1, n)
        def _(step):
            target = lax.rem(me + step, n)
            dispatch(which, me, target).start()

    @pl.loop(1, n)
    def _(step):
        gate_copy(me, lax.rem(me + step, n)).start()

    for copy in own_copies:
        copy.wait()

    def share_out(which, group):
        along(which, group, share, to_far, far).start()
        along(which, group, share, to_near, near).start()

    def pass_on(which, group):
        along(which, group, far, to_far, far).wait_recv()
        along(which, group, far, passed, near).start()

    for which in range(2):
        share_out(which, me)

        @pl.loop(1, n)
        def _(step):
            group = lax.rem(me - step + n, n)
            dispatch(which, group, me).wait_recv()
            share_out(which, group)
            pass_on(which, lax.rem(me - step + 1 + n, n))

        pass_on(which, lax.rem(me + 1, n))
    for which in range(2):

        @pl.loop(0, n)
        def _(group):
            along(which, group, near, to_near, near).wait_recv()
            along(which, group, 3 - share, passed, near).wait_recv()
            along(which, group, share, to_far, far).wait_send()
            along(which, group, share, to_near, near).wait_send()
            along(which, group, far, passed, near).wait_send()

        @pl.loop(1, n)
        def _(step):
            dispatch(which, me, lax.rem(me + step, n)).wait_send()

    @pl.loop(1, n)
    def _(step):
        gate_copy(me, lax.rem(me + step, n)).wait_send()
        gate_copy(lax.rem(me - step + n, n), me).wait_recv()


def spread(send_x, send_dy, send_g):
    n, most, quarter = send_x.shape
    wide = jax.ShapeDtypeStruct((n, most, 4 * quarter), send_x.dtype)
    dma = pltpu.SemaphoreType.DMA
    return pl.pallas_call(
        functools.partial(spread_kernel, n),
        out_shape=(wide, wide, jax.ShapeDtypeStruct(send_g.shape, send_g.dtype)),
        in_specs=[VMEM] * 3,
        out_specs=[VMEM] * 3,
        scratch_shapes=[dma((2 * n,))] * 8 + [dma((n,)), dma((n,)), dma((3,))],
        compiler_params=pltpu.CompilerParams(
            collective_id=0, has_side_effects=True, vmem_limit_bytes=VMEM_BYTES
        ),
    )(send_x, send_dy, send_g)


def collect_kernel(n, c_ref, p_ref, out, grad_out, near_got, far_put, far_got, put, total,
                   part_got, part_sum, *sems):
    me, share, near, far = positions(n)
    quarter = out.shape[2]
    to_near, to_far, back, grads, parts = (sems[2 * i : 2 * i + 2] for i in range(5))
    own = sems[10]

    def cols(which):
        return pl.ds(pl.multiple_of(which * quarter, 128), quarter)

    def half(group, slot):
        wanted = near if slot == 1 else 3 - share
        return remote(
            c_ref.at[group, :, cols(wanted)],
            near_got.at[group, slot],
            to_near,
            group * 2 + slot,
            (me, near),
        )

    def across(group):
        return remote(far_put.at[group], far_got.at[group], to_far, group, (me, far))

    def home(source, target):
        return remote(put.at[target], out.at[source], back, source, (target, share))

    def grad_home(source, target):
        return remote(
            part_sum.at[target], grad_out.at[source], grads, source, (target, share)
        )

    greet(n, me, share, near, far)
    part_near = remote(p_ref, part_got.at[0], parts, 0, (me, near))
    part_near.start()

    @pl.loop(0, n)
    def _(step):
        group = lax.rem(me + 1 + step, n)
        half(group, 0).start()
        half(group, 1).start()

    part_near.wait()
    part_sum[...] = p_ref[...] + part_got[0]
    part_far = remote(part_sum, part_got.at[1], parts, 1, (me, far))
    part_far.start()
    part_far.wait()
    part_sum[...] = part_sum[...] + part_got[1]

    @pl.loop(1, n)
    def _(step):
        grad_home(me, lax.rem(me + step, n)).start()

    def pair_sum(group):
        half(group, 0).wait_recv()
        mine = c_ref[group, :, cols(far)].astype(jnp.float32)
        far_put[group] = (mine + near_got[group, 0].astype(jnp.float32)).astype(far_put.dtype)
        across(group).start()
        half(group, 1).wait_recv()
        mine = c_ref[group, :, cols(share)].astype(jnp.float32)
        total[group] = mine + near_got[group, 1].astype(jnp.float32)

    def full_sum(group):
        across(group).wait_recv()
        put[group] = (total[group] + far_got[group].astype(jnp.float32)).astype(put.dtype)

    def send_home(group):
        full_sum(group)
        home(me, group).start()

    pair_sum(lax.rem(me + 1, n))

    @pl.loop(2, n + 1)
    def _(step):
        pair_sum(lax.rem(me + step, n))
        send_home(lax.rem(me + step - 1, n))

    full_sum(me)
    own_copies = [
        pltpu.make_async_copy(put.at[me], out.at[me], own.at[0]),
        pltpu.make_async_copy(part_sum.at[me], grad_out.at[me], own.at[1]),
    ]
    for copy in own_copies:
        copy.start()
    for copy in own_copies:
        copy.wait()

    @pl.loop(0, n)
    def _(group):
        half(group, 0).wait_send()
        half(group, 1).wait_send()
        across(group).wait_send()

    @pl.loop(1, n)
    def _(step):
        target = lax.rem(me + step, n)
        source = lax.rem(me - step + n, n)
        home(me, target).wait_send()
        grad_home(me, target).wait_send()
        home(source, me).wait_recv()
        grad_home(source, me).wait_recv()


def collect(contrib, partial_grad):
    n, most, width = contrib.shape
    quarter = width // 4
    kind = contrib.dtype
    dma = pltpu.SemaphoreType.DMA
    stage = pltpu.VMEM((n, most, quarter), kind)
    return pl.pallas_call(
        functools.partial(collect_kernel, n),
        out_shape=(
            jax.ShapeDtypeStruct((n, most, quarter), kind),
            jax.ShapeDtypeStruct(partial_grad.shape, partial_grad.dtype),
        ),
        in_specs=[VMEM] * 2,
        out_specs=[VMEM] * 2,
        scratch_shapes=[
            pltpu.VMEM((n, 2, most, quarter), kind),
            stage,
            stage,
            stage,
            pltpu.VMEM((n, most, quarter), jnp.float32),
            pltpu.VMEM((2,) + partial_grad.shape, jnp.float32),
            pltpu.VMEM(partial_grad.shape, jnp.float32),
            dma((2 * n,)),
            dma((2 * n,)),
        ]
        + [dma((n,))] * 6
        + [dma((2,)), dma((2,)), dma((2,))],
        compiler_params=pltpu.CompilerParams(
            collective_id=1, has_side_effects=True, vmem_limit_bytes=VMEM_BYTES
        ),
    )(contrib, partial_grad)


def fused_kernel(n, x_ref, dy_ref, g_ref, gate_hbm, up_hbm, down_hbm, out, grad_out,
                 x_out, dy_out, g_out, gate_w, up_w, down_w, pre, up, dz, dp, du,
                 near_put, mine, near_got, far_put, far_got, put, part, part_got, part_sum,
                 load, *all_sems):
    sems, late = all_sems[:11], all_sems[11:]
    me, share, near, far = positions(n)
    quarter = x_ref.shape[2]
    by_group, to_near, to_far, passed, gates = (sems[2 * i : 2 * i + 2] for i in range(5))
    own = sems[10]
    pairs = ((x_ref, x_out), (dy_ref, dy_out))

    def cols(which):
        return pl.ds(pl.multiple_of(which * quarter, 128), quarter)

    def block(which, group, owner):
        return pairs[which][1].at[group, :, cols(owner)]

    def ahead(place):
        return lax.rem(me + (place + n // 2 - 3) % (n - 1) + 1, n)

    def behind(place):
        return lax.rem(me + n - (place + n // 2 - 3) % (n - 1) - 1, n)

    def dispatch(which, place):
        return remote(
            pairs[which][0].at[ahead(place)],
            block(which, place, share),
            by_group,
            which * n + place,
            (ahead(place), share),
        )

    def gate_copy(place):
        return remote(
            g_ref.at[ahead(place)], g_out.at[place], gates, place, (ahead(place), share)
        )

    def along(which, group, sent, sems_of, peer):
        return remote(
            block(which, group, sent),
            block(which, group, sent),
            sems_of,
            which * n + group,
            (me, peer),
        )

    to_pair, across_sems, back, grads, parts = (late[2 * i : 2 * i + 2] for i in range(5))
    most = x_ref.shape[1]
    rows = n * most
    depth = quarter // 2
    narrow = quarter // 7
    loads = [
        pltpu.make_async_copy(src, dst, load.at[i])
        for i, (src, dst) in enumerate(
            ((gate_hbm, gate_w), (up_hbm, up_w), (down_hbm, down_w))
        )
    ]

    def half(group, slot):
        return remote(
            near_put.at[slot, group],
            near_got.at[slot, group],
            to_pair,
            slot * n + group,
            (me, near),
        )

    def across(group):
        return remote(far_put.at[group], far_got.at[group], across_sems, group, (me, far))

    def home(place, landing):
        return remote(put.at[place], out.at[landing], back, place, (behind(place), share))

    def grad_home(place, landing):
        return remote(
            part_sum.at[place], grad_out.at[landing], grads, place, (behind(place), share)
        )

    def nt(left, right):
        return lax.dot_general(
            left, right, (((1,), (1,)), ((), ())), preferred_element_type=jnp.float32
        )

    few = n // 2

    def lines(part_at):
        return pl.ds(part_at * few * most, few * most)

    def places(part_at):
        return pl.ds(part_at * few, few)

    def project(part_at, first, last):
        @pl.loop(first, last)
        def _(step):
            at = pl.ds(pl.multiple_of(step * depth, 128), depth)
            piece = x_out[places(part_at), :, at].reshape(few * most, depth)
            to = lines(part_at)
            pre[to, :] += jnp.dot(piece, gate_w[at, :], preferred_element_type=jnp.float32)
            up[to, :] += jnp.dot(piece, up_w[at, :], preferred_element_type=jnp.float32)

    def share_out(which, place):
        along(which, place, share, to_far, far).start()
        along(which, place, share, to_near, near).start()

    def pass_on(which, place):
        along(which, place, far, to_far, far).wait_recv()
        along(which, place, far, passed, near).start()

    def accept(which, place):
        if place > 0:
            dispatch(which, place).wait_recv()
        share_out(which, place)
        if place % few > 0:
            pass_on(which, place - 1)

    def settle(which, part_at):
        pass_on(which, part_at * few + few - 1)

        @pl.loop(part_at * few, part_at * few + few)
        def _(place):
            along(which, place, near, to_near, near).wait_recv()
            along(which, place, 3 - share, passed, near).wait_recv()

    def settle_gates(part_at):
        @pl.loop(max(1, part_at * few), part_at * few + few)
        def _(place):
            gate_copy(place).wait_recv()

    def down(part_at):
        @pl.loop(0, 8)
        def _(step):
            at = pl.ds(pl.multiple_of(step * depth, 128), depth)
            piece = dy_out[places(part_at), :, at].reshape(few * most, depth)
            dz[lines(part_at), :] += nt(piece, down_w[:, at])

    def part_near(part_at):
        to = places(part_at)
        return remote(part.at[to], part_got.at[0, to], parts, part_at, (me, near))

    def part_far(part_at):
        to = places(part_at)
        return remote(part_sum.at[to], part_got.at[1, to], parts, 2 + part_at, (me, far))

    def pointwise(part_at):
        @pl.loop(part_at * few, part_at * few + few)
        def _(place):
            at = pl.ds(pl.multiple_of(place * most, 16), most)
            pre_b, up_b, dz_b = pre[at, :], up[at, :], dz[at, :]
            sigma = jax.nn.sigmoid(pre_b)
            active = pre_b * sigma
            row = jnp.sum(active * up_b * dz_b, axis=1, keepdims=True)
            part[place] = jnp.broadcast_to(row, (most, 128))
            scaled = g_out[place][:, :1].astype(jnp.float32) * dz_b
            du[at, :] = (scaled * active).astype(du.dtype)
            dp[at, :] = (scaled * up_b * sigma * (1.0 + pre_b * (1.0 - sigma))).astype(
                dp.dtype
            )

        part_near(part_at).start()

    def expand(part_at, wanted, store):
        @pl.loop(0, 7)
        def _(step):
            at = pl.ds(pl.multiple_of(wanted * quarter + step * narrow, 128), narrow)
            to = lines(part_at)
            value = nt(dp[to, :], gate_w[at, :]) + nt(du[to, :], up_w[at, :])
            store(
                pl.ds(pl.multiple_of(step * narrow, 128), narrow),
                value.reshape(few, most, narrow),
            )

    def for_near(part_at, slot):
        def keep(at, value):
            near_put[slot, places(part_at), :, at] = value.astype(near_put.dtype)

        expand(part_at, 3 - share if slot == 0 else near, keep)

        @pl.loop(part_at * few, part_at * few + few)
        def _(place):
            half(place, slot).start()

    def for_self(part_at, slot):
        def keep(at, value):
            mine[slot, places(part_at), :, at] = value

        expand(part_at, far if slot == 0 else share, keep)

    def send_far(part_at):
        to = places(part_at)
        part_near(part_at).wait()
        part_sum[to] = part[to] + part_got[0, to]
        part_far(part_at).start()

        @pl.loop(part_at * few, part_at * few + few)
        def _(place):
            half(place, 0).wait_recv()
            far_put[place] = (
                mine[0, place] + near_got[0, place].astype(jnp.float32)
            ).astype(far_put.dtype)
            across(place).start()

    def send_grads(part_at):
        to = places(part_at)
        part_far(part_at).wait()
        part_sum[to] = part_sum[to] + part_got[1, to]

        @pl.loop(max(1, part_at * few), part_at * few + few)
        def _(place):
            grad_home(place, me).start()

    def full_sum(place):
        half(place, 1).wait_recv()
        across(place).wait_recv()
        pair = mine[1, place] + near_got[1, place].astype(jnp.float32)
        put[place] = (pair + far_got[place].astype(jnp.float32)).astype(put.dtype)

    def send_home(first, last):
        @pl.loop(first, last)
        def _(place):
            full_sum(place)
            home(place, me).start()

    greet(n, me, share, near, far)
    own_copies = [
        pltpu.make_async_copy(src.at[me], block(which, 0, share), own.at[which])
        for which, (src, _) in enumerate(pairs)
    ]
    own_copies.append(pltpu.make_async_copy(g_ref.at[me], g_out.at[0], own.at[2]))
    for copy in own_copies:
        copy.start()
    for first, last in ((1, few), (few, n)):
        for which in range(2):

            @pl.loop(first, last)
            def _(place):
                dispatch(which, place).start()

        @pl.loop(first, last)
        def _(place):
            gate_copy(place).start()

    for copy in loads:
        copy.start()
    pre[...] = jnp.zeros_like(pre)
    up[...] = jnp.zeros_like(up)
    dz[...] = jnp.zeros_like(dz)
    for copy in own_copies:
        copy.wait()
    for place in range(few):
        accept(0, place)
    accept(1, 0)
    settle(0, 0)
    loads[0].wait()
    loads[1].wait()
    for place in range(1, few):
        project(0, 8 * (place - 1) // (few - 1), 8 * place // (few - 1))
        accept(1, place)
    accept(0, few)
    settle(1, 0)
    settle_gates(0)
    loads[2].wait()
    down(0)
    pointwise(0)
    early = [
        lambda: for_near(0, 0),
        lambda: for_near(0, 1),
        lambda: (for_self(0, 0), send_far(0)),
    ]
    for place in range(few + 1, n):
        accept(0, place)
        early[place - few - 1]()
    accept(1, few)
    settle(0, 1)
    for_self(0, 1)
    for place in range(few + 1, n):
        project(1, 8 * (place - few - 1) // (few - 1), 8 * (place - few) // (few - 1))
        accept(1, place)
        if place == few + 1:
            send_grads(0)
        send_home(place - few, place - few + 1)
    settle(1, 1)
    settle_gates(1)
    down(1)
    pointwise(1)
    for_near(1, 0)
    for_near(1, 1)
    for_self(1, 0)
    send_far(1)
    for_self(1, 1)
    send_grads(1)
    send_home(few, n)
    full_sum(0)
    last_copies = [
        pltpu.make_async_copy(put.at[0], out.at[me], own.at[0]),
        pltpu.make_async_copy(part_sum.at[0], grad_out.at[me], own.at[1]),
    ]
    for copy in last_copies:
        copy.start()
    for copy in last_copies:
        copy.wait()
    for which in range(2):

        @pl.loop(0, n)
        def _(place):
            along(which, place, share, to_far, far).wait_send()
            along(which, place, share, to_near, near).wait_send()
            along(which, place, far, passed, near).wait_send()
            half(place, which).wait_send()

        @pl.loop(1, n)
        def _(place):
            dispatch(which, place).wait_send()

    @pl.loop(0, n)
    def _(place):
        across(place).wait_send()

    @pl.loop(1, n)
    def _(place):
        gate_copy(place).wait_send()
        home(place, me).wait_send()
        grad_home(place, me).wait_send()
        home(place, ahead(place)).wait_recv()
        grad_home(place, ahead(place)).wait_recv()


def fused(send_x, send_dy, send_g, gate_mat, up_mat, down_mat):
    n, most, quarter = send_x.shape
    kind = send_x.dtype
    hidden = gate_mat.shape[1]
    rows = n * most
    dma = pltpu.SemaphoreType.DMA
    wide = pltpu.VMEM((n, most, 4 * quarter), kind)
    square = pltpu.VMEM((rows, hidden), jnp.float32)
    stage = pltpu.VMEM((n, most, quarter), kind)
    flat = (n, most, 128)
    anywhere = pl.BlockSpec(memory_space=pl.ANY)
    return pl.pallas_call(
        functools.partial(fused_kernel, n),
        out_shape=(
            jax.ShapeDtypeStruct((n, most, quarter), kind),
            jax.ShapeDtypeStruct(flat, jnp.float32),
        ),
        in_specs=[VMEM] * 3 + [anywhere] * 3,
        out_specs=[VMEM] * 2,
        scratch_shapes=[
            wide,
            wide,
            pltpu.VMEM(flat, kind),
            pltpu.VMEM(gate_mat.shape, kind),
            pltpu.VMEM(up_mat.shape, kind),
            pltpu.VMEM(down_mat.shape, kind),
            square,
            square,
            square,
            pltpu.VMEM((rows, hidden), kind),
            pltpu.VMEM((rows, hidden), kind),
            pltpu.VMEM((2, n, most, quarter), kind),
            pltpu.VMEM((2, n, most, quarter), jnp.float32),
            pltpu.VMEM((2, n, most, quarter), kind),
            stage,
            stage,
            stage,
            pltpu.VMEM(flat, jnp.float32),
            pltpu.VMEM((2,) + flat, jnp.float32),
            pltpu.VMEM(flat, jnp.float32),
            dma((3,)),
        ]
        + [dma((2 * n,))] * 8
        + [dma((n,)), dma((n,)), dma((3,))]
        + [dma((2 * n,))] * 2
        + [dma((n,))] * 6
        + [dma((4,))] * 2,
        compiler_params=pltpu.CompilerParams(
            collective_id=2, has_side_effects=True, vmem_limit_bytes=VMEM_BYTES
        ),
    )(send_x, send_dy, send_g, gate_mat, up_mat, down_mat)


def in_steps(send_x, send_dy, send_g, gate_mat, up_mat, down_mat):
    n_experts, most_slots, quarter = send_x.shape
    slot_count = n_experts * most_slots
    piece_x, piece_dy, recv_g = spread(
        send_x,
        send_dy,
        send_g.reshape(n_experts, 1, most_slots),
    )
    piece_x = piece_x.reshape(slot_count, 4 * quarter)
    piece_dy = piece_dy.reshape(slot_count, 4 * quarter)
    pre_sum = jnp.dot(piece_x, gate_mat, preferred_element_type=jnp.float32)
    up_sum = jnp.dot(piece_x, up_mat, preferred_element_type=jnp.float32)
    grad_sum = lax.dot_general(
        piece_dy, down_mat, (((1,), (1,)), ((), ())), preferred_element_type=jnp.float32
    )
    sigma = jax.nn.sigmoid(pre_sum)
    active = pre_sum * sigma
    partial_grad = jnp.sum(active * up_sum * grad_sum, axis=1)
    weight_g = recv_g.reshape(slot_count)
    scaled = weight_g[:, None] * grad_sum
    grad_up = (scaled * active).astype(jnp.bfloat16)
    grad_pre = (scaled * up_sum * sigma * (1.0 + pre_sum * (1.0 - sigma))).astype(jnp.bfloat16)
    contrib = lax.dot_general(
        grad_pre, gate_mat, (((1,), (1,)), ((), ())), preferred_element_type=jnp.float32
    )
    contrib = contrib + lax.dot_general(
        grad_up, up_mat, (((1,), (1,)), ((), ())), preferred_element_type=jnp.float32
    )
    returned, returned_grad = collect(
        contrib.astype(jnp.bfloat16).reshape(n_experts, most_slots, 4 * quarter),
        partial_grad.reshape(n_experts, 1, most_slots),
    )
    return returned, returned_grad


def local(tokens, out_grad, expert_ids, gate_values, w_gate, w_up, w_down):
    n_experts = lax.axis_size("expert")
    tok_rows, quarter = tokens.shape
    top_count = expert_ids.shape[1]
    most_slots = 3 * tok_rows * top_count // (2 * n_experts)
    slot_count = n_experts * most_slots
    flat_ids = expert_ids.reshape(-1)
    onehot = (flat_ids[:, None] == jnp.arange(n_experts, dtype=jnp.int32)[None, :]).astype(
        jnp.int32
    )
    before = jnp.cumsum(onehot, axis=0) - onehot
    rank = jnp.sum(before * onehot, axis=1)
    slot_of = (flat_ids * most_slots + rank).reshape(tok_rows, top_count)
    matches = slot_of[None, :, :] == jnp.arange(slot_count, dtype=jnp.int32)[:, None, None]
    chooser = jnp.any(matches, axis=2).astype(jnp.bfloat16)
    send_x = jnp.dot(chooser, tokens, preferred_element_type=jnp.float32).astype(jnp.bfloat16)
    send_dy = jnp.dot(chooser, out_grad, preferred_element_type=jnp.float32).astype(jnp.bfloat16)
    gate_wide = gate_values.astype(jnp.float32)[None, :, :]
    send_g = jnp.sum(jnp.where(matches, gate_wide, 0.0), axis=(1, 2))
    send_x = send_x.reshape(n_experts, most_slots, quarter)
    send_dy = send_dy.reshape(n_experts, most_slots, quarter)
    weights = (w_gate[0], w_up[0], w_down[0])
    if most_slots % 16 == 0 and n_experts == 8 and quarter % 1792 == 0:
        wide_g = jnp.broadcast_to(
            send_g.astype(jnp.bfloat16).reshape(n_experts, most_slots, 1),
            (n_experts, most_slots, 128),
        )
        returned, returned_grad = fused(send_x, send_dy, wide_g, *weights)
        returned_grad = returned_grad[:, :, 0]
    else:
        returned, returned_grad = in_steps(send_x, send_dy, send_g, *weights)
    d_tokens = lax.dot_general(
        chooser,
        returned.reshape(slot_count, quarter),
        (((0,), (0,)), ((), ())),
        preferred_element_type=jnp.float32,
    ).astype(jnp.bfloat16)
    grad_wide = returned_grad.reshape(slot_count)[:, None, None]
    d_gates = jnp.sum(jnp.where(matches, grad_wide, 0.0), axis=0)
    return (d_tokens, d_gates)


def solution(mesh):
    placed = (
        P("expert", "tensor"),
        P("expert", "tensor"),
        P("expert", None),
        P("expert", None),
        P("expert", None, "tensor"),
        P("expert", None, "tensor"),
        P("expert", "tensor", None),
    )
    return jax.shard_map(
        local,
        mesh=mesh,
        in_specs=placed,
        out_specs=(P("expert", "tensor"), P("expert", None)),
        check_vma=False,
    )
```

```python
import functools

import jax
import jax.numpy as jnp
from jax import lax
from jax.experimental import pallas as pl
from jax.experimental.pallas import tpu as pltpu
from jax.sharding import PartitionSpec as P


MESH = pl.DeviceIdType.MESH
VMEM = pl.BlockSpec(memory_space=pltpu.VMEM)
VMEM_BYTES = 56 * 1024 * 1024


def positions(n):
    me = lax.axis_index("expert")
    share = lax.axis_index("tensor")
    pair, side = share // 2, share % 2
    return me, share, pair * 2 + 1 - side, (1 - pair) * 2 + side


def greet(n, me, share, near, far):
    barrier = pltpu.get_barrier_semaphore()

    @pl.loop(1, n)
    def _(step):
        pl.semaphore_signal(
            barrier, inc=1, device_id=(lax.rem(me + step, n), share), device_id_type=MESH
        )

    for peer in (near, far):
        pl.semaphore_signal(barrier, inc=1, device_id=(me, peer), device_id_type=MESH)
    pl.semaphore_wait(barrier, n + 1)


def remote(src, dst, sems, index, device):
    return pltpu.make_async_remote_copy(
        src_ref=src,
        dst_ref=dst,
        send_sem=sems[0].at[index],
        recv_sem=sems[1].at[index],
        device_id=device,
        device_id_type=MESH,
    )


def spread_kernel(n, x_ref, dy_ref, g_ref, x_out, dy_out, g_out, *sems):
    me, share, near, far = positions(n)
    quarter = x_ref.shape[2]
    by_group, to_near, to_far, passed, gates = (sems[2 * i : 2 * i + 2] for i in range(5))
    own = sems[10]
    pairs = ((x_ref, x_out), (dy_ref, dy_out))

    def cols(which):
        return pl.ds(pl.multiple_of(which * quarter, 128), quarter)

    def block(which, group, owner):
        return pairs[which][1].at[group, :, cols(owner)]

    def dispatch(which, source, target):
        return remote(
            pairs[which][0].at[target],
            block(which, source, share),
            by_group,
            which * n + source,
            (target, share),
        )

    def gate_copy(source, target):
        return remote(
            g_ref.at[target], g_out.at[source], gates, source, (target, share)
        )

    def along(which, group, sent, sems_of, peer):
        return remote(
            block(which, group, sent),
            block(which, group, sent),
            sems_of,
            which * n + group,
            (me, peer),
        )

    greet(n, me, share, near, far)
    own_copies = [
        pltpu.make_async_copy(src.at[me], block(which, me, share), own.at[which])
        for which, (src, _) in enumerate(pairs)
    ]
    own_copies.append(pltpu.make_async_copy(g_ref.at[me], g_out.at[me], own.at[2]))
    for copy in own_copies:
        copy.start()
    for which in range(2):

        @pl.loop(1, n)
        def _(step):
            target = lax.rem(me + step, n)
            dispatch(which, me, target).start()

    @pl.loop(1, n)
    def _(step):
        gate_copy(me, lax.rem(me + step, n)).start()

    for copy in own_copies:
        copy.wait()

    def share_out(which, group):
        along(which, group, share, to_far, far).start()
        along(which, group, share, to_near, near).start()

    def pass_on(which, group):
        along(which, group, far, to_far, far).wait_recv()
        along(which, group, far, passed, near).start()

    for which in range(2):
        share_out(which, me)

        @pl.loop(1, n)
        def _(step):
            group = lax.rem(me - step + n, n)
            dispatch(which, group, me).wait_recv()
            share_out(which, group)
            pass_on(which, lax.rem(me - step + 1 + n, n))

        pass_on(which, lax.rem(me + 1, n))
    for which in range(2):

        @pl.loop(0, n)
        def _(group):
            along(which, group, near, to_near, near).wait_recv()
            along(which, group, 3 - share, passed, near).wait_recv()
            along(which, group, share, to_far, far).wait_send()
            along(which, group, share, to_near, near).wait_send()
            along(which, group, far, passed, near).wait_send()

        @pl.loop(1, n)
        def _(step):
            dispatch(which, me, lax.rem(me + step, n)).wait_send()

    @pl.loop(1, n)
    def _(step):
        gate_copy(me, lax.rem(me + step, n)).wait_send()
        gate_copy(lax.rem(me - step + n, n), me).wait_recv()


def spread(send_x, send_dy, send_g):
    n, most, quarter = send_x.shape
    wide = jax.ShapeDtypeStruct((n, most, 4 * quarter), send_x.dtype)
    dma = pltpu.SemaphoreType.DMA
    return pl.pallas_call(
        functools.partial(spread_kernel, n),
        out_shape=(wide, wide, jax.ShapeDtypeStruct(send_g.shape, send_g.dtype)),
        in_specs=[VMEM] * 3,
        out_specs=[VMEM] * 3,
        scratch_shapes=[dma((2 * n,))] * 8 + [dma((n,)), dma((n,)), dma((3,))],
        compiler_params=pltpu.CompilerParams(
            collective_id=0, has_side_effects=True, vmem_limit_bytes=VMEM_BYTES
        ),
    )(send_x, send_dy, send_g)


def collect_kernel(n, c_ref, p_ref, out, grad_out, near_got, far_put, far_got, put, total,
                   part_got, part_sum, *sems):
    me, share, near, far = positions(n)
    quarter = out.shape[2]
    to_near, to_far, back, grads, parts = (sems[2 * i : 2 * i + 2] for i in range(5))
    own = sems[10]

    def cols(which):
        return pl.ds(pl.multiple_of(which * quarter, 128), quarter)

    def half(group, slot):
        wanted = near if slot == 1 else 3 - share
        return remote(
            c_ref.at[group, :, cols(wanted)],
            near_got.at[group, slot],
            to_near,
            group * 2 + slot,
            (me, near),
        )

    def across(group):
        return remote(far_put.at[group], far_got.at[group], to_far, group, (me, far))

    def home(source, target):
        return remote(put.at[target], out.at[source], back, source, (target, share))

    def grad_home(source, target):
        return remote(
            part_sum.at[target], grad_out.at[source], grads, source, (target, share)
        )

    greet(n, me, share, near, far)
    part_near = remote(p_ref, part_got.at[0], parts, 0, (me, near))
    part_near.start()

    @pl.loop(0, n)
    def _(step):
        group = lax.rem(me + 1 + step, n)
        half(group, 0).start()
        half(group, 1).start()

    part_near.wait()
    part_sum[...] = p_ref[...] + part_got[0]
    part_far = remote(part_sum, part_got.at[1], parts, 1, (me, far))
    part_far.start()
    part_far.wait()
    part_sum[...] = part_sum[...] + part_got[1]

    @pl.loop(1, n)
    def _(step):
        grad_home(me, lax.rem(me + step, n)).start()

    def pair_sum(group):
        half(group, 0).wait_recv()
        mine = c_ref[group, :, cols(far)].astype(jnp.float32)
        far_put[group] = (mine + near_got[group, 0].astype(jnp.float32)).astype(far_put.dtype)
        across(group).start()
        half(group, 1).wait_recv()
        mine = c_ref[group, :, cols(share)].astype(jnp.float32)
        total[group] = mine + near_got[group, 1].astype(jnp.float32)

    def full_sum(group):
        across(group).wait_recv()
        put[group] = (total[group] + far_got[group].astype(jnp.float32)).astype(put.dtype)

    def send_home(group):
        full_sum(group)
        home(me, group).start()

    pair_sum(lax.rem(me + 1, n))

    @pl.loop(2, n + 1)
    def _(step):
        pair_sum(lax.rem(me + step, n))
        send_home(lax.rem(me + step - 1, n))

    full_sum(me)
    own_copies = [
        pltpu.make_async_copy(put.at[me], out.at[me], own.at[0]),
        pltpu.make_async_copy(part_sum.at[me], grad_out.at[me], own.at[1]),
    ]
    for copy in own_copies:
        copy.start()
    for copy in own_copies:
        copy.wait()

    @pl.loop(0, n)
    def _(group):
        half(group, 0).wait_send()
        half(group, 1).wait_send()
        across(group).wait_send()

    @pl.loop(1, n)
    def _(step):
        target = lax.rem(me + step, n)
        source = lax.rem(me - step + n, n)
        home(me, target).wait_send()
        grad_home(me, target).wait_send()
        home(source, me).wait_recv()
        grad_home(source, me).wait_recv()


def collect(contrib, partial_grad):
    n, most, width = contrib.shape
    quarter = width // 4
    kind = contrib.dtype
    dma = pltpu.SemaphoreType.DMA
    stage = pltpu.VMEM((n, most, quarter), kind)
    return pl.pallas_call(
        functools.partial(collect_kernel, n),
        out_shape=(
            jax.ShapeDtypeStruct((n, most, quarter), kind),
            jax.ShapeDtypeStruct(partial_grad.shape, partial_grad.dtype),
        ),
        in_specs=[VMEM] * 2,
        out_specs=[VMEM] * 2,
        scratch_shapes=[
            pltpu.VMEM((n, 2, most, quarter), kind),
            stage,
            stage,
            stage,
            pltpu.VMEM((n, most, quarter), jnp.float32),
            pltpu.VMEM((2,) + partial_grad.shape, jnp.float32),
            pltpu.VMEM(partial_grad.shape, jnp.float32),
            dma((2 * n,)),
            dma((2 * n,)),
        ]
        + [dma((n,))] * 6
        + [dma((2,)), dma((2,)), dma((2,))],
        compiler_params=pltpu.CompilerParams(
            collective_id=1, has_side_effects=True, vmem_limit_bytes=VMEM_BYTES
        ),
    )(contrib, partial_grad)


def fused_kernel(n, x_ref, dy_ref, g_ref, gate_hbm, up_hbm, down_hbm, out, grad_out,
                 x_out, dy_out, g_out, gate_w, up_w, down_w, pre, up, dz, dp, du,
                 near_put, mine, near_got, far_put, far_got, put, part, part_got, part_sum,
                 load, *all_sems):
    sems, late = all_sems[:11], all_sems[11:]
    me, share, near, far = positions(n)
    quarter = x_ref.shape[2]
    by_group, to_near, to_far, passed, gates = (sems[2 * i : 2 * i + 2] for i in range(5))
    own = sems[10]
    pairs = ((x_ref, x_out), (dy_ref, dy_out))

    def cols(which):
        return pl.ds(pl.multiple_of(which * quarter, 128), quarter)

    def block(which, group, owner):
        return pairs[which][1].at[group, :, cols(owner)]

    shift = (share % 2) * (n // 2 - 1)

    def ahead(step):
        return lax.rem(me + (step - 1 + shift) % (n - 1) + 1, n)

    def behind(step):
        return lax.rem(me + n - (step - 1 + shift) % (n - 1) - 1, n)

    def dispatch(which, source, target):
        return remote(
            pairs[which][0].at[target],
            block(which, source, share),
            by_group,
            which * n + source,
            (target, share),
        )

    def gate_copy(source, target):
        return remote(
            g_ref.at[target], g_out.at[source], gates, source, (target, share)
        )

    def along(which, group, sent, sems_of, peer):
        return remote(
            block(which, group, sent),
            block(which, group, sent),
            sems_of,
            which * n + group,
            (me, peer),
        )

    to_pair, across_sems, back, grads, parts = (late[2 * i : 2 * i + 2] for i in range(5))
    most = x_ref.shape[1]
    rows = n * most
    depth = quarter // 2
    narrow = quarter // 7
    loads = [
        pltpu.make_async_copy(src, dst, load.at[i])
        for i, (src, dst) in enumerate(
            ((gate_hbm, gate_w), (up_hbm, up_w), (down_hbm, down_w))
        )
    ]

    def half(group, slot):
        return remote(
            near_put.at[slot, group],
            near_got.at[slot, group],
            to_pair,
            slot * n + group,
            (me, near),
        )

    def across(group):
        return remote(far_put.at[group], far_got.at[group], across_sems, group, (me, far))

    def home(source, target):
        return remote(put.at[target], out.at[source], back, source, (target, share))

    def grad_home(source, target):
        return remote(
            part_sum.at[target], grad_out.at[source], grads, source, (target, share)
        )

    def nt(left, right):
        return lax.dot_general(
            left, right, (((1,), (1,)), ((), ())), preferred_element_type=jnp.float32
        )

    def project(step):
        at = pl.ds(pl.multiple_of(step * depth, 128), depth)
        piece = x_out[:, :, at].reshape(rows, depth)
        pre[...] += jnp.dot(piece, gate_w[at, :], preferred_element_type=jnp.float32)
        up[...] += jnp.dot(piece, up_w[at, :], preferred_element_type=jnp.float32)

    greet(n, me, share, near, far)
    own_copies = [
        pltpu.make_async_copy(src.at[me], block(which, me, share), own.at[which])
        for which, (src, _) in enumerate(pairs)
    ]
    own_copies.append(pltpu.make_async_copy(g_ref.at[me], g_out.at[me], own.at[2]))
    for copy in own_copies:
        copy.start()
    for which in range(2):

        @pl.loop(1, n)
        def _(step):
            dispatch(which, me, ahead(step)).start()

    @pl.loop(1, n)
    def _(step):
        gate_copy(me, lax.rem(me + step, n)).start()

    for copy in loads:
        copy.start()
    pre[...] = jnp.zeros_like(pre)
    up[...] = jnp.zeros_like(up)
    dz[...] = jnp.zeros_like(dz)
    for copy in own_copies:
        copy.wait()

    def share_out(which, group):
        along(which, group, share, to_far, far).start()
        along(which, group, share, to_near, near).start()

    def pass_on(which, group):
        along(which, group, far, to_far, far).wait_recv()
        along(which, group, far, passed, near).start()

    def settle(which):
        @pl.loop(0, n)
        def _(group):
            along(which, group, near, to_near, near).wait_recv()
            along(which, group, 3 - share, passed, near).wait_recv()

    share_out(0, me)

    @pl.loop(1, n)
    def _(step):
        dispatch(0, behind(step), me).wait_recv()
        share_out(0, behind(step))

        @pl.when(step > 1)
        def _():
            pass_on(0, behind(step - 1 + (n - 1)))

    share_out(1, me)
    pass_on(0, me)
    pass_on(0, behind(n - 1))
    settle(0)
    loads[0].wait()
    loads[1].wait()

    @pl.loop(1, n)
    def _(step):
        project(step - 1)
        dispatch(1, behind(step), me).wait_recv()
        share_out(1, behind(step))

        @pl.when(step > 1)
        def _():
            pass_on(1, behind(step - 1 + (n - 1)))

    @pl.loop(n - 1, 8)
    def _(step):
        project(step)

    pass_on(1, me)
    pass_on(1, behind(n - 1))

    @pl.loop(1, n)
    def _(step):
        gate_copy(lax.rem(me - step + n, n), me).wait_recv()

    loads[2].wait()
    settle(1)

    @pl.loop(0, 8)
    def _(step):
        at = pl.ds(pl.multiple_of(step * depth, 128), depth)
        dz[...] += nt(dy_out[:, :, at].reshape(rows, depth), down_w[:, at])

    @pl.loop(0, n)
    def _(group):
        at = pl.ds(pl.multiple_of(group * most, 16), most)
        pre_b, up_b, dz_b = pre[at, :], up[at, :], dz[at, :]
        sigma = jax.nn.sigmoid(pre_b)
        active = pre_b * sigma
        row = jnp.sum(active * up_b * dz_b, axis=1, keepdims=True)
        part[group] = jnp.broadcast_to(row, (most, 128))
        scaled = g_out[group][:, :1].astype(jnp.float32) * dz_b
        du[at, :] = (scaled * active).astype(du.dtype)
        dp[at, :] = (scaled * up_b * sigma * (1.0 + pre_b * (1.0 - sigma))).astype(dp.dtype)

    part_near = remote(part, part_got.at[0], parts, 0, (me, near))
    part_near.start()

    def expand(which, store):
        @pl.loop(0, 7)
        def _(step):
            at = pl.ds(pl.multiple_of(which * quarter + step * narrow, 128), narrow)
            value = nt(dp[...], gate_w[at, :]) + nt(du[...], up_w[at, :])
            store(
                pl.ds(pl.multiple_of(step * narrow, 128), narrow),
                value.reshape(n, most, narrow),
            )

    for slot, wanted in ((0, 3 - share), (1, near)):

        def keep(at, value):
            near_put[slot, :, :, at] = value.astype(near_put.dtype)

        expand(wanted, keep)

        @pl.loop(0, n)
        def _(step):
            half(lax.rem(me + 1 + step, n), slot).start()

    for slot, wanted in ((0, far), (1, share)):

        def keep_wide(at, value):
            mine[slot, :, :, at] = value

        expand(wanted, keep_wide)
        if slot == 0:
            part_near.wait()
            part_sum[...] = part[...] + part_got[0]
            part_far = remote(part_sum, part_got.at[1], parts, 1, (me, far))
            part_far.start()

            def send_far(group):
                half(group, 0).wait_recv()
                far_put[group] = (
                    mine[0, group] + near_got[0, group].astype(jnp.float32)
                ).astype(far_put.dtype)
                across(group).start()

            @pl.loop(1, n)
            def _(step):
                send_far(ahead(step))

            send_far(me)

    part_far.wait()
    part_sum[...] = part_sum[...] + part_got[1]

    @pl.loop(1, n)
    def _(step):
        grad_home(me, lax.rem(me + step, n)).start()

    def full_sum(group):
        half(group, 1).wait_recv()
        across(group).wait_recv()
        pair = mine[1, group] + near_got[1, group].astype(jnp.float32)
        put[group] = (pair + far_got[group].astype(jnp.float32)).astype(put.dtype)

    @pl.loop(1, n)
    def _(step):
        full_sum(ahead(step))
        home(me, ahead(step)).start()

    full_sum(me)
    last_copies = [
        pltpu.make_async_copy(put.at[me], out.at[me], own.at[0]),
        pltpu.make_async_copy(part_sum.at[me], grad_out.at[me], own.at[1]),
    ]
    for copy in last_copies:
        copy.start()
    for copy in last_copies:
        copy.wait()
    for which in range(2):

        @pl.loop(0, n)
        def _(group):
            along(which, group, share, to_far, far).wait_send()
            along(which, group, share, to_near, near).wait_send()
            along(which, group, far, passed, near).wait_send()
            half(group, which).wait_send()

        @pl.loop(1, n)
        def _(step):
            dispatch(which, me, lax.rem(me + step, n)).wait_send()

    @pl.loop(0, n)
    def _(group):
        across(group).wait_send()

    @pl.loop(1, n)
    def _(step):
        target = lax.rem(me + step, n)
        source = lax.rem(me - step + n, n)
        gate_copy(me, target).wait_send()
        home(me, target).wait_send()
        grad_home(me, target).wait_send()
        home(source, me).wait_recv()
        grad_home(source, me).wait_recv()


def fused(send_x, send_dy, send_g, gate_mat, up_mat, down_mat):
    n, most, quarter = send_x.shape
    kind = send_x.dtype
    hidden = gate_mat.shape[1]
    rows = n * most
    dma = pltpu.SemaphoreType.DMA
    wide = pltpu.VMEM((n, most, 4 * quarter), kind)
    square = pltpu.VMEM((rows, hidden), jnp.float32)
    stage = pltpu.VMEM((n, most, quarter), kind)
    flat = (n, most, 128)
    anywhere = pl.BlockSpec(memory_space=pl.ANY)
    return pl.pallas_call(
        functools.partial(fused_kernel, n),
        out_shape=(
            jax.ShapeDtypeStruct((n, most, quarter), kind),
            jax.ShapeDtypeStruct(flat, jnp.float32),
        ),
        in_specs=[VMEM] * 3 + [anywhere] * 3,
        out_specs=[VMEM] * 2,
        scratch_shapes=[
            wide,
            wide,
            pltpu.VMEM(flat, kind),
            pltpu.VMEM(gate_mat.shape, kind),
            pltpu.VMEM(up_mat.shape, kind),
            pltpu.VMEM(down_mat.shape, kind),
            square,
            square,
            square,
            pltpu.VMEM((rows, hidden), kind),
            pltpu.VMEM((rows, hidden), kind),
            pltpu.VMEM((2, n, most, quarter), kind),
            pltpu.VMEM((2, n, most, quarter), jnp.float32),
            pltpu.VMEM((2, n, most, quarter), kind),
            stage,
            stage,
            stage,
            pltpu.VMEM(flat, jnp.float32),
            pltpu.VMEM((2,) + flat, jnp.float32),
            pltpu.VMEM(flat, jnp.float32),
            dma((3,)),
        ]
        + [dma((2 * n,))] * 8
        + [dma((n,)), dma((n,)), dma((3,))]
        + [dma((2 * n,))] * 2
        + [dma((n,))] * 6
        + [dma((2,))] * 2,
        compiler_params=pltpu.CompilerParams(
            collective_id=2, has_side_effects=True, vmem_limit_bytes=VMEM_BYTES
        ),
    )(send_x, send_dy, send_g, gate_mat, up_mat, down_mat)


def in_steps(send_x, send_dy, send_g, gate_mat, up_mat, down_mat):
    n_experts, most_slots, quarter = send_x.shape
    slot_count = n_experts * most_slots
    piece_x, piece_dy, recv_g = spread(
        send_x,
        send_dy,
        send_g.reshape(n_experts, 1, most_slots),
    )
    piece_x = piece_x.reshape(slot_count, 4 * quarter)
    piece_dy = piece_dy.reshape(slot_count, 4 * quarter)
    pre_sum = jnp.dot(piece_x, gate_mat, preferred_element_type=jnp.float32)
    up_sum = jnp.dot(piece_x, up_mat, preferred_element_type=jnp.float32)
    grad_sum = lax.dot_general(
        piece_dy, down_mat, (((1,), (1,)), ((), ())), preferred_element_type=jnp.float32
    )
    sigma = jax.nn.sigmoid(pre_sum)
    active = pre_sum * sigma
    partial_grad = jnp.sum(active * up_sum * grad_sum, axis=1)
    weight_g = recv_g.reshape(slot_count)
    scaled = weight_g[:, None] * grad_sum
    grad_up = (scaled * active).astype(jnp.bfloat16)
    grad_pre = (scaled * up_sum * sigma * (1.0 + pre_sum * (1.0 - sigma))).astype(jnp.bfloat16)
    contrib = lax.dot_general(
        grad_pre, gate_mat, (((1,), (1,)), ((), ())), preferred_element_type=jnp.float32
    )
    contrib = contrib + lax.dot_general(
        grad_up, up_mat, (((1,), (1,)), ((), ())), preferred_element_type=jnp.float32
    )
    returned, returned_grad = collect(
        contrib.astype(jnp.bfloat16).reshape(n_experts, most_slots, 4 * quarter),
        partial_grad.reshape(n_experts, 1, most_slots),
    )
    return returned, returned_grad


def local(tokens, out_grad, expert_ids, gate_values, w_gate, w_up, w_down):
    n_experts = lax.axis_size("expert")
    tok_rows, quarter = tokens.shape
    top_count = expert_ids.shape[1]
    most_slots = 3 * tok_rows * top_count // (2 * n_experts)
    slot_count = n_experts * most_slots
    flat_ids = expert_ids.reshape(-1)
    onehot = (flat_ids[:, None] == jnp.arange(n_experts, dtype=jnp.int32)[None, :]).astype(
        jnp.int32
    )
    before = jnp.cumsum(onehot, axis=0) - onehot
    rank = jnp.sum(before * onehot, axis=1)
    slot_of = (flat_ids * most_slots + rank).reshape(tok_rows, top_count)
    matches = slot_of[None, :, :] == jnp.arange(slot_count, dtype=jnp.int32)[:, None, None]
    chooser = jnp.any(matches, axis=2).astype(jnp.bfloat16)
    send_x = jnp.dot(chooser, tokens, preferred_element_type=jnp.float32).astype(jnp.bfloat16)
    send_dy = jnp.dot(chooser, out_grad, preferred_element_type=jnp.float32).astype(jnp.bfloat16)
    gate_wide = gate_values.astype(jnp.float32)[None, :, :]
    send_g = jnp.sum(jnp.where(matches, gate_wide, 0.0), axis=(1, 2))
    send_x = send_x.reshape(n_experts, most_slots, quarter)
    send_dy = send_dy.reshape(n_experts, most_slots, quarter)
    weights = (w_gate[0], w_up[0], w_down[0])
    if most_slots % 16 == 0 and n_experts <= 9 and quarter % 1792 == 0:
        wide_g = jnp.broadcast_to(
            send_g.astype(jnp.bfloat16).reshape(n_experts, most_slots, 1),
            (n_experts, most_slots, 128),
        )
        returned, returned_grad = fused(send_x, send_dy, wide_g, *weights)
        returned_grad = returned_grad[:, :, 0]
    else:
        returned, returned_grad = in_steps(send_x, send_dy, send_g, *weights)
    d_tokens = lax.dot_general(
        chooser,
        returned.reshape(slot_count, quarter),
        (((0,), (0,)), ((), ())),
        preferred_element_type=jnp.float32,
    ).astype(jnp.bfloat16)
    grad_wide = returned_grad.reshape(slot_count)[:, None, None]
    d_gates = jnp.sum(jnp.where(matches, grad_wide, 0.0), axis=0)
    return (d_tokens, d_gates)


def solution(mesh):
    placed = (
        P("expert", "tensor"),
        P("expert", "tensor"),
        P("expert", None),
        P("expert", None),
        P("expert", None, "tensor"),
        P("expert", None, "tensor"),
        P("expert", "tensor", None),
    )
    return jax.shard_map(
        local,
        mesh=mesh,
        in_specs=placed,
        out_specs=(P("expert", "tensor"), P("expert", None)),
        check_vma=False,
    )
```

```python
import functools

import jax
import jax.numpy as jnp
from jax import lax
from jax.experimental import pallas as pl
from jax.experimental.pallas import tpu as pltpu
from jax.sharding import PartitionSpec as P


MESH = pl.DeviceIdType.MESH
VMEM = pl.BlockSpec(memory_space=pltpu.VMEM)
VMEM_BYTES = 56 * 1024 * 1024


def positions(n):
    me = lax.axis_index("expert")
    share = lax.axis_index("tensor")
    pair, side = share // 2, share % 2
    return me, share, pair * 2 + 1 - side, (1 - pair) * 2 + side


def greet(n, me, share, near, far):
    barrier = pltpu.get_barrier_semaphore()

    @pl.loop(1, n)
    def _(step):
        pl.semaphore_signal(
            barrier, inc=1, device_id=(lax.rem(me + step, n), share), device_id_type=MESH
        )

    for peer in (near, far):
        pl.semaphore_signal(barrier, inc=1, device_id=(me, peer), device_id_type=MESH)
    pl.semaphore_wait(barrier, n + 1)


def remote(src, dst, sems, index, device):
    return pltpu.make_async_remote_copy(
        src_ref=src,
        dst_ref=dst,
        send_sem=sems[0].at[index],
        recv_sem=sems[1].at[index],
        device_id=device,
        device_id_type=MESH,
    )


def spread_kernel(n, x_ref, dy_ref, g_ref, x_out, dy_out, g_out, *sems):
    me, share, near, far = positions(n)
    quarter = x_ref.shape[2]
    by_group, to_near, to_far, passed, gates = (sems[2 * i : 2 * i + 2] for i in range(5))
    own = sems[10]
    pairs = ((x_ref, x_out), (dy_ref, dy_out))

    def cols(which):
        return pl.ds(pl.multiple_of(which * quarter, 128), quarter)

    def block(which, group, owner):
        return pairs[which][1].at[group, :, cols(owner)]

    def dispatch(which, source, target):
        return remote(
            pairs[which][0].at[target],
            block(which, source, share),
            by_group,
            which * n + source,
            (target, share),
        )

    def gate_copy(source, target):
        return remote(
            g_ref.at[target], g_out.at[source], gates, source, (target, share)
        )

    def along(which, group, sent, sems_of, peer):
        return remote(
            block(which, group, sent),
            block(which, group, sent),
            sems_of,
            which * n + group,
            (me, peer),
        )

    greet(n, me, share, near, far)
    own_copies = [
        pltpu.make_async_copy(src.at[me], block(which, me, share), own.at[which])
        for which, (src, _) in enumerate(pairs)
    ]
    own_copies.append(pltpu.make_async_copy(g_ref.at[me], g_out.at[me], own.at[2]))
    for copy in own_copies:
        copy.start()
    for which in range(2):

        @pl.loop(1, n)
        def _(step):
            target = lax.rem(me + step, n)
            dispatch(which, me, target).start()

    @pl.loop(1, n)
    def _(step):
        gate_copy(me, lax.rem(me + step, n)).start()

    for copy in own_copies:
        copy.wait()

    def share_out(which, group):
        along(which, group, share, to_far, far).start()
        along(which, group, share, to_near, near).start()

    def pass_on(which, group):
        along(which, group, far, to_far, far).wait_recv()
        along(which, group, far, passed, near).start()

    for which in range(2):
        share_out(which, me)

        @pl.loop(1, n)
        def _(step):
            group = lax.rem(me - step + n, n)
            dispatch(which, group, me).wait_recv()
            share_out(which, group)
            pass_on(which, lax.rem(me - step + 1 + n, n))

        pass_on(which, lax.rem(me + 1, n))
    for which in range(2):

        @pl.loop(0, n)
        def _(group):
            along(which, group, near, to_near, near).wait_recv()
            along(which, group, 3 - share, passed, near).wait_recv()
            along(which, group, share, to_far, far).wait_send()
            along(which, group, share, to_near, near).wait_send()
            along(which, group, far, passed, near).wait_send()

        @pl.loop(1, n)
        def _(step):
            dispatch(which, me, lax.rem(me + step, n)).wait_send()

    @pl.loop(1, n)
    def _(step):
        gate_copy(me, lax.rem(me + step, n)).wait_send()
        gate_copy(lax.rem(me - step + n, n), me).wait_recv()


def spread(send_x, send_dy, send_g):
    n, most, quarter = send_x.shape
    wide = jax.ShapeDtypeStruct((n, most, 4 * quarter), send_x.dtype)
    dma = pltpu.SemaphoreType.DMA
    return pl.pallas_call(
        functools.partial(spread_kernel, n),
        out_shape=(wide, wide, jax.ShapeDtypeStruct(send_g.shape, send_g.dtype)),
        in_specs=[VMEM] * 3,
        out_specs=[VMEM] * 3,
        scratch_shapes=[dma((2 * n,))] * 8 + [dma((n,)), dma((n,)), dma((3,))],
        compiler_params=pltpu.CompilerParams(
            collective_id=0, has_side_effects=True, vmem_limit_bytes=VMEM_BYTES
        ),
    )(send_x, send_dy, send_g)


def collect_kernel(n, c_ref, p_ref, out, grad_out, near_got, far_put, far_got, put, total,
                   part_got, part_sum, *sems):
    me, share, near, far = positions(n)
    quarter = out.shape[2]
    to_near, to_far, back, grads, parts = (sems[2 * i : 2 * i + 2] for i in range(5))
    own = sems[10]

    def cols(which):
        return pl.ds(pl.multiple_of(which * quarter, 128), quarter)

    def half(group, slot):
        wanted = near if slot == 1 else 3 - share
        return remote(
            c_ref.at[group, :, cols(wanted)],
            near_got.at[group, slot],
            to_near,
            group * 2 + slot,
            (me, near),
        )

    def across(group):
        return remote(far_put.at[group], far_got.at[group], to_far, group, (me, far))

    def home(source, target):
        return remote(put.at[target], out.at[source], back, source, (target, share))

    def grad_home(source, target):
        return remote(
            part_sum.at[target], grad_out.at[source], grads, source, (target, share)
        )

    greet(n, me, share, near, far)
    part_near = remote(p_ref, part_got.at[0], parts, 0, (me, near))
    part_near.start()

    @pl.loop(0, n)
    def _(step):
        group = lax.rem(me + 1 + step, n)
        half(group, 0).start()
        half(group, 1).start()

    part_near.wait()
    part_sum[...] = p_ref[...] + part_got[0]
    part_far = remote(part_sum, part_got.at[1], parts, 1, (me, far))
    part_far.start()
    part_far.wait()
    part_sum[...] = part_sum[...] + part_got[1]

    @pl.loop(1, n)
    def _(step):
        grad_home(me, lax.rem(me + step, n)).start()

    def pair_sum(group):
        half(group, 0).wait_recv()
        mine = c_ref[group, :, cols(far)].astype(jnp.float32)
        far_put[group] = (mine + near_got[group, 0].astype(jnp.float32)).astype(far_put.dtype)
        across(group).start()
        half(group, 1).wait_recv()
        mine = c_ref[group, :, cols(share)].astype(jnp.float32)
        total[group] = mine + near_got[group, 1].astype(jnp.float32)

    def full_sum(group):
        across(group).wait_recv()
        put[group] = (total[group] + far_got[group].astype(jnp.float32)).astype(put.dtype)

    def send_home(group):
        full_sum(group)
        home(me, group).start()

    pair_sum(lax.rem(me + 1, n))

    @pl.loop(2, n + 1)
    def _(step):
        pair_sum(lax.rem(me + step, n))
        send_home(lax.rem(me + step - 1, n))

    full_sum(me)
    own_copies = [
        pltpu.make_async_copy(put.at[me], out.at[me], own.at[0]),
        pltpu.make_async_copy(part_sum.at[me], grad_out.at[me], own.at[1]),
    ]
    for copy in own_copies:
        copy.start()
    for copy in own_copies:
        copy.wait()

    @pl.loop(0, n)
    def _(group):
        half(group, 0).wait_send()
        half(group, 1).wait_send()
        across(group).wait_send()

    @pl.loop(1, n)
    def _(step):
        target = lax.rem(me + step, n)
        source = lax.rem(me - step + n, n)
        home(me, target).wait_send()
        grad_home(me, target).wait_send()
        home(source, me).wait_recv()
        grad_home(source, me).wait_recv()


def collect(contrib, partial_grad):
    n, most, width = contrib.shape
    quarter = width // 4
    kind = contrib.dtype
    dma = pltpu.SemaphoreType.DMA
    stage = pltpu.VMEM((n, most, quarter), kind)
    return pl.pallas_call(
        functools.partial(collect_kernel, n),
        out_shape=(
            jax.ShapeDtypeStruct((n, most, quarter), kind),
            jax.ShapeDtypeStruct(partial_grad.shape, partial_grad.dtype),
        ),
        in_specs=[VMEM] * 2,
        out_specs=[VMEM] * 2,
        scratch_shapes=[
            pltpu.VMEM((n, 2, most, quarter), kind),
            stage,
            stage,
            stage,
            pltpu.VMEM((n, most, quarter), jnp.float32),
            pltpu.VMEM((2,) + partial_grad.shape, jnp.float32),
            pltpu.VMEM(partial_grad.shape, jnp.float32),
            dma((2 * n,)),
            dma((2 * n,)),
        ]
        + [dma((n,))] * 6
        + [dma((2,)), dma((2,)), dma((2,))],
        compiler_params=pltpu.CompilerParams(
            collective_id=1, has_side_effects=True, vmem_limit_bytes=VMEM_BYTES
        ),
    )(contrib, partial_grad)


def fused_kernel(n, tok_ref, grad_ref, pick_ref, g_ref, gate_hbm, up_hbm, down_hbm, out, grad_out,
                 x_ref, dy_ref, x_out, dy_out, g_out, gate_w, up_w, down_w, pre, up, dz, dp, du,
                 near_put, mine, near_got, far_put, far_got, put, part, part_got, part_sum,
                 load, *all_sems):
    sems, late = all_sems[:11], all_sems[11:]
    me, share, near, far = positions(n)
    quarter = x_ref.shape[2]
    by_group, to_near, to_far, passed, gates = (sems[2 * i : 2 * i + 2] for i in range(5))
    own = sems[10]
    pairs = ((x_ref, x_out), (dy_ref, dy_out))

    def cols(which):
        return pl.ds(pl.multiple_of(which * quarter, 128), quarter)

    def block(which, group, owner):
        return pairs[which][1].at[group, :, cols(owner)]

    def dispatch(which, source, target):
        return remote(
            pairs[which][0].at[target],
            block(which, source, share),
            by_group,
            which * n + source,
            (target, share),
        )

    def gate_copy(source, target):
        return remote(
            g_ref.at[target], g_out.at[source], gates, source, (target, share)
        )

    def along(which, group, sent, sems_of, peer):
        return remote(
            block(which, group, sent),
            block(which, group, sent),
            sems_of,
            which * n + group,
            (me, peer),
        )

    to_pair, across_sems, back, grads, parts = (late[2 * i : 2 * i + 2] for i in range(5))
    most = x_ref.shape[1]
    rows = n * most
    depth = quarter // 2
    narrow = quarter // 7
    loads = [
        pltpu.make_async_copy(src, dst, load.at[i])
        for i, (src, dst) in enumerate(
            ((gate_hbm, gate_w), (up_hbm, up_w), (down_hbm, down_w))
        )
    ]

    def half(group, slot):
        return remote(
            near_put.at[slot, group],
            near_got.at[slot, group],
            to_pair,
            slot * n + group,
            (me, near),
        )

    def across(group):
        return remote(far_put.at[group], far_got.at[group], across_sems, group, (me, far))

    def home(source, target):
        return remote(put.at[target], out.at[source], back, source, (target, share))

    def grad_home(source, target):
        return remote(
            part_sum.at[target], grad_out.at[source], grads, source, (target, share)
        )

    def nt(left, right):
        return lax.dot_general(
            left, right, (((1,), (1,)), ((), ())), preferred_element_type=jnp.float32
        )

    def project(step):
        at = pl.ds(pl.multiple_of(step * depth, 128), depth)
        piece = x_out[:, :, at].reshape(rows, depth)
        pre[...] += jnp.dot(piece, gate_w[at, :], preferred_element_type=jnp.float32)
        up[...] += jnp.dot(piece, up_w[at, :], preferred_element_type=jnp.float32)

    greet(n, me, share, near, far)
    own_copies = [pltpu.make_async_copy(g_ref.at[me], g_out.at[me], own.at[2])]
    for copy in own_copies:
        copy.start()

    def picked(which, target):
        rows_of = (tok_ref, grad_ref)[which]
        return jnp.dot(
            pick_ref[target], rows_of[...], preferred_element_type=jnp.float32
        ).astype(x_ref.dtype)

    for which in range(2):

        @pl.loop(1, n)
        def _(step):
            target = lax.rem(me + step, n)
            pairs[which][0][target] = picked(which, target)
            dispatch(which, me, target).start()

        pairs[which][1][me, :, cols(share)] = picked(which, me)

    @pl.loop(1, n)
    def _(step):
        gate_copy(me, lax.rem(me + step, n)).start()

    for copy in loads:
        copy.start()
    pre[...] = jnp.zeros_like(pre)
    up[...] = jnp.zeros_like(up)
    dz[...] = jnp.zeros_like(dz)
    for copy in own_copies:
        copy.wait()

    def share_out(which, group):
        along(which, group, share, to_far, far).start()
        along(which, group, share, to_near, near).start()

    def pass_on(which, group):
        along(which, group, far, to_far, far).wait_recv()
        along(which, group, far, passed, near).start()

    def settle(which):
        @pl.loop(0, n)
        def _(group):
            along(which, group, near, to_near, near).wait_recv()
            along(which, group, 3 - share, passed, near).wait_recv()

    share_out(0, me)

    @pl.loop(1, n)
    def _(step):
        group = lax.rem(me - step + n, n)
        dispatch(0, group, me).wait_recv()
        share_out(0, group)
        pass_on(0, lax.rem(me - step + 1 + n, n))

    share_out(1, me)
    pass_on(0, lax.rem(me + 1, n))
    settle(0)
    loads[0].wait()
    loads[1].wait()

    @pl.loop(1, n)
    def _(step):
        project(step - 1)
        group = lax.rem(me - step + n, n)
        dispatch(1, group, me).wait_recv()
        share_out(1, group)
        pass_on(1, lax.rem(me - step + 1 + n, n))

    @pl.loop(n - 1, 8)
    def _(step):
        project(step)

    pass_on(1, lax.rem(me + 1, n))

    @pl.loop(1, n)
    def _(step):
        gate_copy(lax.rem(me - step + n, n), me).wait_recv()

    loads[2].wait()
    settle(1)

    @pl.loop(0, 8)
    def _(step):
        at = pl.ds(pl.multiple_of(step * depth, 128), depth)
        dz[...] += nt(dy_out[:, :, at].reshape(rows, depth), down_w[:, at])

    @pl.loop(0, n)
    def _(group):
        at = pl.ds(pl.multiple_of(group * most, 16), most)
        pre_b, up_b, dz_b = pre[at, :], up[at, :], dz[at, :]
        sigma = jax.nn.sigmoid(pre_b)
        active = pre_b * sigma
        row = jnp.sum(active * up_b * dz_b, axis=1, keepdims=True)
        part[group] = jnp.broadcast_to(row, (most, 128))
        scaled = g_out[group][:, :1].astype(jnp.float32) * dz_b
        du[at, :] = (scaled * active).astype(du.dtype)
        dp[at, :] = (scaled * up_b * sigma * (1.0 + pre_b * (1.0 - sigma))).astype(dp.dtype)

    part_near = remote(part, part_got.at[0], parts, 0, (me, near))
    part_near.start()

    def expand(which, store):
        @pl.loop(0, 7)
        def _(step):
            at = pl.ds(pl.multiple_of(which * quarter + step * narrow, 128), narrow)
            value = nt(dp[...], gate_w[at, :]) + nt(du[...], up_w[at, :])
            store(
                pl.ds(pl.multiple_of(step * narrow, 128), narrow),
                value.reshape(n, most, narrow),
            )

    for slot, wanted in ((0, 3 - share), (1, near)):

        def keep(at, value):
            near_put[slot, :, :, at] = value.astype(near_put.dtype)

        expand(wanted, keep)

        @pl.loop(0, n)
        def _(step):
            half(lax.rem(me + 1 + step, n), slot).start()

    for slot, wanted in ((0, far), (1, share)):

        def keep_wide(at, value):
            mine[slot, :, :, at] = value

        expand(wanted, keep_wide)
        if slot == 0:
            part_near.wait()
            part_sum[...] = part[...] + part_got[0]
            part_far = remote(part_sum, part_got.at[1], parts, 1, (me, far))
            part_far.start()

            @pl.loop(0, n)
            def _(step):
                group = lax.rem(me + 1 + step, n)
                half(group, 0).wait_recv()
                far_put[group] = (
                    mine[0, group] + near_got[0, group].astype(jnp.float32)
                ).astype(far_put.dtype)
                across(group).start()

    part_far.wait()
    part_sum[...] = part_sum[...] + part_got[1]

    @pl.loop(1, n)
    def _(step):
        grad_home(me, lax.rem(me + step, n)).start()

    def full_sum(group):
        half(group, 1).wait_recv()
        across(group).wait_recv()
        pair = mine[1, group] + near_got[1, group].astype(jnp.float32)
        put[group] = (pair + far_got[group].astype(jnp.float32)).astype(put.dtype)

    @pl.loop(1, n)
    def _(step):
        group = lax.rem(me + step, n)
        full_sum(group)
        home(me, group).start()

    full_sum(me)
    last_copies = [
        pltpu.make_async_copy(put.at[me], out.at[me], own.at[0]),
        pltpu.make_async_copy(part_sum.at[me], grad_out.at[me], own.at[1]),
    ]
    for copy in last_copies:
        copy.start()
    for copy in last_copies:
        copy.wait()
    for which in range(2):

        @pl.loop(0, n)
        def _(group):
            along(which, group, share, to_far, far).wait_send()
            along(which, group, share, to_near, near).wait_send()
            along(which, group, far, passed, near).wait_send()
            half(group, which).wait_send()

        @pl.loop(1, n)
        def _(step):
            dispatch(which, me, lax.rem(me + step, n)).wait_send()

    @pl.loop(0, n)
    def _(group):
        across(group).wait_send()

    @pl.loop(1, n)
    def _(step):
        target = lax.rem(me + step, n)
        source = lax.rem(me - step + n, n)
        gate_copy(me, target).wait_send()
        home(me, target).wait_send()
        grad_home(me, target).wait_send()
        home(source, me).wait_recv()
        grad_home(source, me).wait_recv()


def fused(tokens, out_grad, chooser, send_g, gate_mat, up_mat, down_mat):
    n, most, _ = chooser.shape
    quarter = tokens.shape[1]
    kind = tokens.dtype
    hidden = gate_mat.shape[1]
    rows = n * most
    dma = pltpu.SemaphoreType.DMA
    wide = pltpu.VMEM((n, most, 4 * quarter), kind)
    square = pltpu.VMEM((rows, hidden), jnp.float32)
    stage = pltpu.VMEM((n, most, quarter), kind)
    flat = (n, most, 128)
    anywhere = pl.BlockSpec(memory_space=pl.ANY)
    return pl.pallas_call(
        functools.partial(fused_kernel, n),
        out_shape=(
            jax.ShapeDtypeStruct((n, most, quarter), kind),
            jax.ShapeDtypeStruct(flat, jnp.float32),
        ),
        in_specs=[VMEM] * 4 + [anywhere] * 3,
        out_specs=[VMEM] * 2,
        scratch_shapes=[
            stage,
            stage,
            wide,
            wide,
            pltpu.VMEM(flat, kind),
            pltpu.VMEM(gate_mat.shape, kind),
            pltpu.VMEM(up_mat.shape, kind),
            pltpu.VMEM(down_mat.shape, kind),
            square,
            square,
            square,
            pltpu.VMEM((rows, hidden), kind),
            pltpu.VMEM((rows, hidden), kind),
            pltpu.VMEM((2, n, most, quarter), kind),
            pltpu.VMEM((2, n, most, quarter), jnp.float32),
            pltpu.VMEM((2, n, most, quarter), kind),
            stage,
            stage,
            stage,
            pltpu.VMEM(flat, jnp.float32),
            pltpu.VMEM((2,) + flat, jnp.float32),
            pltpu.VMEM(flat, jnp.float32),
            dma((3,)),
        ]
        + [dma((2 * n,))] * 8
        + [dma((n,)), dma((n,)), dma((3,))]
        + [dma((2 * n,))] * 2
        + [dma((n,))] * 6
        + [dma((2,))] * 2,
        compiler_params=pltpu.CompilerParams(
            collective_id=2, has_side_effects=True, vmem_limit_bytes=VMEM_BYTES
        ),
    )(tokens, out_grad, chooser, send_g, gate_mat, up_mat, down_mat)


def in_steps(send_x, send_dy, send_g, gate_mat, up_mat, down_mat):
    n_experts, most_slots, quarter = send_x.shape
    slot_count = n_experts * most_slots
    piece_x, piece_dy, recv_g = spread(
        send_x,
        send_dy,
        send_g.reshape(n_experts, 1, most_slots),
    )
    piece_x = piece_x.reshape(slot_count, 4 * quarter)
    piece_dy = piece_dy.reshape(slot_count, 4 * quarter)
    pre_sum = jnp.dot(piece_x, gate_mat, preferred_element_type=jnp.float32)
    up_sum = jnp.dot(piece_x, up_mat, preferred_element_type=jnp.float32)
    grad_sum = lax.dot_general(
        piece_dy, down_mat, (((1,), (1,)), ((), ())), preferred_element_type=jnp.float32
    )
    sigma = jax.nn.sigmoid(pre_sum)
    active = pre_sum * sigma
    partial_grad = jnp.sum(active * up_sum * grad_sum, axis=1)
    weight_g = recv_g.reshape(slot_count)
    scaled = weight_g[:, None] * grad_sum
    grad_up = (scaled * active).astype(jnp.bfloat16)
    grad_pre = (scaled * up_sum * sigma * (1.0 + pre_sum * (1.0 - sigma))).astype(jnp.bfloat16)
    contrib = lax.dot_general(
        grad_pre, gate_mat, (((1,), (1,)), ((), ())), preferred_element_type=jnp.float32
    )
    contrib = contrib + lax.dot_general(
        grad_up, up_mat, (((1,), (1,)), ((), ())), preferred_element_type=jnp.float32
    )
    returned, returned_grad = collect(
        contrib.astype(jnp.bfloat16).reshape(n_experts, most_slots, 4 * quarter),
        partial_grad.reshape(n_experts, 1, most_slots),
    )
    return returned, returned_grad


def local(tokens, out_grad, expert_ids, gate_values, w_gate, w_up, w_down):
    n_experts = lax.axis_size("expert")
    tok_rows, quarter = tokens.shape
    top_count = expert_ids.shape[1]
    most_slots = 3 * tok_rows * top_count // (2 * n_experts)
    slot_count = n_experts * most_slots
    flat_ids = expert_ids.reshape(-1)
    onehot = (flat_ids[:, None] == jnp.arange(n_experts, dtype=jnp.int32)[None, :]).astype(
        jnp.int32
    )
    before = jnp.cumsum(onehot, axis=0) - onehot
    rank = jnp.sum(before * onehot, axis=1)
    slot_of = (flat_ids * most_slots + rank).reshape(tok_rows, top_count)
    matches = slot_of[None, :, :] == jnp.arange(slot_count, dtype=jnp.int32)[:, None, None]
    chooser = jnp.any(matches, axis=2).astype(jnp.bfloat16)
    send_x = jnp.dot(chooser, tokens, preferred_element_type=jnp.float32).astype(jnp.bfloat16)
    send_dy = jnp.dot(chooser, out_grad, preferred_element_type=jnp.float32).astype(jnp.bfloat16)
    gate_wide = gate_values.astype(jnp.float32)[None, :, :]
    send_g = jnp.sum(jnp.where(matches, gate_wide, 0.0), axis=(1, 2))
    send_x = send_x.reshape(n_experts, most_slots, quarter)
    send_dy = send_dy.reshape(n_experts, most_slots, quarter)
    weights = (w_gate[0], w_up[0], w_down[0])
    if most_slots % 16 == 0 and n_experts <= 9 and quarter % 1792 == 0:
        wide_g = jnp.broadcast_to(
            send_g.astype(jnp.bfloat16).reshape(n_experts, most_slots, 1),
            (n_experts, most_slots, 128),
        )
        returned, returned_grad = fused(
            tokens,
            out_grad,
            chooser.reshape(n_experts, most_slots, tok_rows),
            wide_g,
            *weights,
        )
        returned_grad = returned_grad[:, :, 0]
    else:
        returned, returned_grad = in_steps(send_x, send_dy, send_g, *weights)
    d_tokens = lax.dot_general(
        chooser,
        returned.reshape(slot_count, quarter),
        (((0,), (0,)), ((), ())),
        preferred_element_type=jnp.float32,
    ).astype(jnp.bfloat16)
    grad_wide = returned_grad.reshape(slot_count)[:, None, None]
    d_gates = jnp.sum(jnp.where(matches, grad_wide, 0.0), axis=0)
    return (d_tokens, d_gates)


def solution(mesh):
    placed = (
        P("expert", "tensor"),
        P("expert", "tensor"),
        P("expert", None),
        P("expert", None),
        P("expert", None, "tensor"),
        P("expert", None, "tensor"),
        P("expert", "tensor", None),
    )
    return jax.shard_map(
        local,
        mesh=mesh,
        in_specs=placed,
        out_specs=(P("expert", "tensor"), P("expert", None)),
        check_vma=False,
    )
```
